128 devices in a mesh: lat: 4 (over z_lo, core), lon: 32 (over x, z_hi, y).
Axes of the slice: x: 4, y: 4, z: 4 (z_hi: 2, z_lo: 2; z = z_hi * 2 + z_lo), core: 2. Of those that a mesh axis runs over, the one named last changes fastest.
Arguments:
- cell_state: bfloat16 [4, 32, 512, 32, 64], P('lat', 'lon'), may hold values from -6 to 6
- remap_weight: bfloat16 [4, 32, 512, 64, 128], P('lat', 'lon'), may hold values from -0.75 to 0.75
- block_target: int32 [4, 32, 512], P('lat', 'lon'), may hold values from 0 to 255, as said below
- block_count: int32 [4, 32], P('lat', 'lon'), may hold values from 256 to 512, as said below
- border_state: bfloat16 [4, 32, 128, 32, 64], P('lat', 'lon'), may hold values from -6 to 6
- border_weight: bfloat16 [4, 32, 128, 64, 128], P('lat', 'lon'), may hold values from -0.75 to 0.75
- border_target: int32 [4, 32, 128], P('lat', 'lon'), may hold values from 0 to 63
- kernel_one: bfloat16 [7, 7, 32, 64], replicated, may hold values from -0.15625 to 0.15625
- bias_one: float32 [64], replicated, may hold values from -4 to 4
- gain_one: float32 [64], replicated, may hold values from 0.1 to 1.9
- kernel_two: bfloat16 [7, 7, 64, 128], replicated, may hold values from -0.109375 to 0.109375
- bias_two: float32 [128], replicated, may hold values from -4 to 4
- gain_two: float32 [128], replicated, may hold values from 0.1 to 1.9
Outputs:
- encoded: bfloat16 [256, 1024, 128], P('lat', 'lon')
The draws below stay inside these ranges and needn't reach their ends.
Inputs may be any that keep to these rules, and one draw needn't show every extreme that they name: `block_count`: slots below a device's count are live; the largest count is exactly 512 in every draw. `block_target`: on every device, slots 0 to 255 name each patch of the tile once, in an order drawn from the seed; later slots name patches at random.
All inputs are finite; a program needn't handle non-finite values.
Results may differ from the reference program's by a relative error of at most 0.0045.
Values may be sent and summed in bfloat16 or wider, within the bound.
No kernel may reach another device: no remote copies, remote signals or barrier semaphores. Data moves between devices by JAX's collectives and lax.ppermute only.
A program may use at most 192 MiB of HBM per device.

```python
import jax
import jax.numpy as jnp
from jax import lax

C = 32
C1 = 64
C2 = 128
BC = 64
PH = 8
PW = 16
EDGE = 1
TH = 256
W = 128
NB = 512
P_SIZE = 128
PR = 32
PC = 8
NP = 256
EP = 32
NS = 128
BANDS = 4
SECTORS = 32
ROWS = 1024
COLS = 4096


def draw_block_count(key, part):
    band_no = jnp.arange(BANDS, dtype=jnp.int32)[:, None] + jnp.zeros((1, SECTORS), jnp.int32)
    is_polar = (band_no == 0) | (band_no == BANDS - 1)
    spread = NB - NP
    factors = jax.random.randint(jax.random.fold_in(key, 11), (3, BANDS, SECTORS), 0, 9)
    extra_slots = factors[0] * factors[1] * factors[2] * spread // 512
    polar_extra = factors[0] * (spread // 8) // 8
    counts = NP + jnp.where(is_polar, polar_extra, extra_slots)
    return counts.at[BANDS // 2, 0].set(NB).astype(jnp.int32)


def draw_block_target(key, part):
    key_list = jax.random.split(jax.random.fold_in(key, 23), BANDS * SECTORS)
    orders = jax.vmap(lambda one_key: jax.random.permutation(one_key, NP))(key_list)
    remaining = jax.random.randint(jax.random.fold_in(key, 29), (BANDS * SECTORS, NB - NP), 0, NP)
    joined = jnp.concatenate([orders.astype(jnp.int32), remaining.astype(jnp.int32)], 1)
    return joined.reshape(BANDS, SECTORS, NB)


def set_ends(result, own_key, least, top_value):
    extent = result.shape
    spot = [jax.random.randint(jax.random.fold_in(own_key, axis), (), 0, extent[axis]) for axis in range(len(extent))]
    result = result.at[tuple(spot)].set(least)
    longest = extent.index(max(extent))
    spot[longest] = (spot[longest] + 1) % extent[longest]
    return result.at[tuple(spot)].set(top_value)


def level_of(stream_key, shape, cuts, low, largest):
    def one(dim, parts):
        heights = jax.random.uniform(jax.random.fold_in(jax.random.fold_in(stream_key, 6), dim), (parts,), jnp.float32, low / len(cuts), largest / len(cuts))
        return jnp.repeat(jnp.exp(heights), shape[dim] // parts).reshape((-1,) + (1,) * (len(shape) - dim - 1))

    factor_of = one(*cuts[0])
    for cut in cuts[1:]:
        factor_of = factor_of * one(*cut)
    return factor_of


def noise(own_key, dims, deviation, reach, cuts=(), kind=jnp.bfloat16):
    values = deviation * jax.random.normal(own_key, dims, jnp.float32)
    if cuts:
        values = values * level_of(own_key, dims, cuts, -0.22, 0.18)
    return jnp.clip(values, -reach, reach).astype(kind)


def setup_inputs(seed: int = 0) -> dict:
    splits = jax.random.split(jax.random.key(seed), 14)
    cell_state = noise(splits[0], (BANDS, SECTORS, NB, C, BC), 1.0, 6.0, ((0, 4), (1, 32)))
    remap_weight = noise(splits[1], (BANDS, SECTORS, NB, BC, P_SIZE), BC ** -0.5, 0.75, ((0, 4), (1, 32)))
    block_target = draw_block_target(jax.random.fold_in(splits[13], 71), 0)
    block_count = draw_block_count(jax.random.fold_in(splits[13], 71), 0)
    border_state = noise(splits[4], (BANDS, SECTORS, NS, C, BC), 1.0, 6.0, ((0, 4), (1, 32)))
    border_weight = noise(splits[5], (BANDS, SECTORS, NS, BC, P_SIZE), BC ** -0.5, 0.75, ((0, 4), (1, 32)))
    border_target = set_ends(jax.random.randint(splits[6], (BANDS, SECTORS, NS), 0, 2 * EP), jax.random.fold_in(splits[6], 1), 0, (2 * EP) - 1).astype(jnp.int32)
    kernel_one = noise(splits[7], (7, 7, C, C1), (49 * C) ** -0.5, 0.15625)
    bias_one = noise(splits[8], (C1,), 1.0, 4.0, (), jnp.float32)
    gain_one = jnp.clip(1.0 + 0.18 * jax.random.normal(splits[9], (C1,), jnp.float32), 0.1, 1.9)
    kernel_two = noise(splits[10], (7, 7, C1, C2), (49 * C1) ** -0.5, 0.109375)
    bias_two = noise(splits[11], (C2,), 1.0, 4.0, (), jnp.float32)
    gain_two = jnp.clip(1.0 + 0.18 * jax.random.normal(splits[12], (C2,), jnp.float32), 0.1, 1.9)
    return dict(cell_state=cell_state, remap_weight=remap_weight, block_target=block_target, block_count=block_count, border_state=border_state, border_weight=border_weight, border_target=border_target, kernel_one=kernel_one, bias_one=bias_one, gain_one=gain_one, kernel_two=kernel_two, bias_two=bias_two, gain_two=gain_two)


def to_image(totals, row_count, col_count):
    channels = totals.shape[1]
    shaped = totals.reshape(row_count, col_count, channels, PH, PW)
    return shaped.transpose(2, 0, 3, 1, 4).reshape(channels, row_count * PH, col_count * PW)

def block_sums(states, weights, slot_index, segments):
    products = jnp.einsum('ncb,nbp->ncp', states.astype(jnp.float32), weights.astype(jnp.float32), precision=lax.Precision.HIGHEST)
    return jax.ops.segment_sum(products, slot_index, num_segments=segments + 1)[:segments]

def pole_pad(raster):
    half_turn = raster.shape[2] // 2
    upper = jnp.roll(raster[:, :3][:, ::-1], half_turn, axis=2)
    bottom = jnp.roll(raster[:, -3:][:, ::-1], half_turn, axis=2)
    heightened = jnp.concatenate([upper, raster, bottom], 1)
    return jnp.concatenate([heightened[:, :, -3:], heightened, heightened[:, :, :3]], 2)

def conv_layer(raster, kernel, bias_term, gain_term, band_rows, channels_last):
    padded = pole_pad(raster)
    layout = ('NCHW', 'HWIO', 'NHWC') if channels_last else ('NCHW', 'HWIO', 'NCHW')
    results = []
    for band_no in range(BANDS):
        band_piece = padded[:, band_no * band_rows:band_no * band_rows + band_rows + 6].astype(jnp.float32)[None]
        conv_out = lax.conv_general_dilated(band_piece, kernel.astype(jnp.float32), (2, 2), 'VALID', dimension_numbers=layout, precision=lax.Precision.HIGHEST)[0]
        if channels_last:
            conv_out = conv_out + bias_term
            scaled = conv_out * lax.rsqrt(lax.optimization_barrier(jnp.mean(conv_out * conv_out, axis=-1, keepdims=True)) + 1e-05) * gain_term
        else:
            conv_out = conv_out + bias_term[:, None, None]
            scaled = conv_out * lax.rsqrt(lax.optimization_barrier(jnp.mean(conv_out * conv_out, axis=0, keepdims=True)) + 1e-05) * gain_term[:, None, None]
        results.append(jax.nn.gelu(scaled, approximate=True).astype(jnp.bfloat16))
    return jnp.concatenate(results, 0 if channels_last else 1)

def reference(cell_state, remap_weight, block_target, block_count, border_state, border_weight, border_target, kernel_one, bias_one, gain_one, kernel_two, bias_two, gain_two):
    slot_numbers = jnp.arange(NB, dtype=jnp.int32)

    def tile_field(device_flat):
        band_no = device_flat // SECTORS
        sector = device_flat % SECTORS
        west_sector = (sector + SECTORS - 1) % SECTORS
        east_sector = (sector + 1) % SECTORS
        slot_index = jnp.where(slot_numbers < block_count[band_no, sector], block_target[band_no, sector], NP).astype(jnp.int32)
        inner = block_sums(cell_state[band_no, sector], remap_weight[band_no, sector], slot_index, NP)
        from_west = block_sums(border_state[band_no, west_sector], border_weight[band_no, west_sector], border_target[band_no, west_sector], 2 * EP)[EP:]
        from_east = block_sums(border_state[band_no, east_sector], border_weight[band_no, east_sector], border_target[band_no, east_sector], 2 * EP)[:EP]
        raster = to_image(inner, PR, PC)
        raster = raster.at[:, :, :EDGE * PW].add(to_image(from_west, PR, EDGE))
        raster = raster.at[:, :, W - EDGE * PW:].add(to_image(from_east, PR, EDGE))
        return raster.astype(jnp.bfloat16)
    tiles = lax.map(tile_field, jnp.arange(BANDS * SECTORS, dtype=jnp.int32))
    field = tiles.reshape(BANDS, SECTORS, C, TH, W).transpose(2, 0, 3, 1, 4).reshape(C, ROWS, COLS)
    hidden = conv_layer(field, kernel_one, bias_one, gain_one, TH, False)
    return conv_layer(hidden, kernel_two, bias_two, gain_two, TH // 2, True)
```

```python
import functools

import jax
import jax.numpy as jnp
from jax import lax
from jax.experimental import pallas as pl
from jax.experimental.pallas import tpu as pltpu
from jax.sharding import PartitionSpec as P

F32 = jnp.float32
BF16 = jnp.bfloat16
BANDS = 4
SECTORS = 32
EDGE_ROWS = 10


def mesh_pairs(partner):
    return [
        (b * SECTORS + s, (lambda t: t[0] * SECTORS + t[1] % SECTORS)(partner(b, s)))
        for b in range(BANDS)
        for s in range(SECTORS)
    ]


LON_EVEN = mesh_pairs(lambda b, s: (b, s ^ 1))
LON_ODD = mesh_pairs(lambda b, s: (b, s + 1 if s % 2 else s - 1))
LAT_OUTER = mesh_pairs(
    lambda b, s: {0: (0, s + 16), 1: (2, s), 2: (1, s), 3: (3, s + 16)}[b]
)
LAT_INNER = mesh_pairs(lambda b, s: (b ^ 1, s))


def exchange(block, pairs):
    return lax.ppermute(block, ("lat", "lon"), pairs)


def nt_dot(a, b):
    return lax.dot_general(a, b, (((1,), (1,)), ((), ())), preferred_element_type=F32)


def group_ones(size, width):
    rows = lax.broadcasted_iota(jnp.int32, (size, size), 0) // width
    cols = lax.broadcasted_iota(jnp.int32, (size, size), 1) // width
    return (rows == cols).astype(F32).astype(BF16)


def norm_gelu(v, gain, ones, width):
    sq = v * v
    hi = sq.astype(BF16)
    lo = (sq - hi.astype(F32)).astype(BF16)
    total = jnp.dot(hi, ones, preferred_element_type=F32)
    total = total + jnp.dot(lo, ones, preferred_element_type=F32)
    x = v * lax.rsqrt(total * (1.0 / width) + 1e-05) * gain
    return jax.nn.gelu(x, approximate=True)


STEP = 64
UNROLL = 16


def sums_kernel(
    target, count, btarget, bs_ref, bw_ref, s_ref, w_ref, acc_ref, m0_ref, m1_ref, bacc
):
    i = pl.program_id(0)
    odd = lax.axis_index("lon") % 2

    @pl.when(i == 0)
    def _():
        bacc[...] = jnp.zeros_like(bacc)

    def products(sr, wr, n0):
        return [
            jnp.dot(sr[n0 + u], wr[n0 + u], preferred_element_type=F32) for u in range(UNROLL)
        ]

    @pl.when(i < 2)
    def _():
        def body(j, c):
            vals = products(bs_ref, bw_ref, j * UNROLL)
            for u in range(UNROLL):
                t = btarget[i * STEP + j * UNROLL + u]
                bacc[t] += vals[u]
            return c

        lax.fori_loop(0, STEP // UNROLL, body, 0)

    @pl.when((i >= 2) & (i < 6))
    def _():
        def body(j, c):
            vals = products(s_ref, w_ref, j * UNROLL)
            for u in range(UNROLL):
                t = target[(i - 2) * STEP + j * UNROLL + u]
                acc_ref[t] = vals[u]
            return c

        lax.fori_loop(0, STEP // UNROLL, body, 0)

    @pl.when(i >= 6)
    def _():
        def body(j, c):
            vals = products(s_ref, w_ref, j * UNROLL)
            for u in range(UNROLL):
                n = (i - 2) * STEP + j * UNROLL + u
                t = jnp.where(n < count[0], target[n], 256)
                acc_ref[t] += vals[u]
            return c

        lax.fori_loop(0, STEP // UNROLL, body, 0)

    @pl.when(i == pl.num_programs(0) - 1)
    def _():
        def fill(east_ref, west_ref):
            east_ref[0:32] = bacc[32:64].astype(BF16)
            west_ref[0:32] = bacc[0:32].astype(BF16)
            for q in range(32):
                east_ref[32 + q] = acc_ref[8 * q + 7].astype(BF16)
                west_ref[32 + q] = acc_ref[8 * q].astype(BF16)

        @pl.when(odd == 0)
        def _():
            fill(m0_ref, m1_ref)

        @pl.when(odd == 1)
        def _():
            fill(m1_ref, m0_ref)


def block_sums(target, count, btarget, bstate, bweight, state, weight):
    smem = pl.BlockSpec(memory_space=pltpu.SMEM)
    border = lambda i: (jnp.minimum(i, 1), 0, 0)
    inner = lambda i: (jnp.maximum(i - 2, 0), 0, 0)
    whole = lambda i: (0, 0, 0)
    return pl.pallas_call(
        sums_kernel,
        name="block_sums",
        grid=(10,),
        in_specs=[
            smem,
            smem,
            smem,
            pl.BlockSpec((STEP, 32, 64), border),
            pl.BlockSpec((STEP, 64, 128), border),
            pl.BlockSpec((STEP, 32, 64), inner),
            pl.BlockSpec((STEP, 64, 128), inner),
        ],
        out_specs=[
            pl.BlockSpec((257, 32, 128), whole),
            pl.BlockSpec((64, 32, 128), whole),
            pl.BlockSpec((64, 32, 128), whole),
        ],
        out_shape=[
            jax.ShapeDtypeStruct((257, 32, 128), F32),
            jax.ShapeDtypeStruct((64, 32, 128), BF16),
            jax.ShapeDtypeStruct((64, 32, 128), BF16),
        ],
        scratch_shapes=[pltpu.VMEM((64, 32, 128), F32)],
        compiler_params=pltpu.CompilerParams(vmem_limit_bytes=28 << 20),
    )(target, count, btarget, bstate, bweight, state, weight)


def weights_kernel(k1_ref, k2_ref, w1_ref, w2_ref):
    w1_ref[...] = jnp.zeros_like(w1_ref)
    w2_ref[...] = jnp.zeros_like(w2_ref)
    for r in range(7):
        for s in range(7):
            for t in range(4):
                row = r * 512 + (2 * t + s + 1) * 32
                w1_ref[row : row + 32, t * 64 : (t + 1) * 64] = k1_ref[r * 7 + s]
            for t in range(2):
                row = r * 640 + (2 * t + s + 1) * 64
                w2_ref[row : row + 64, t * 128 : (t + 1) * 128] = k2_ref[r * 7 + s]


def matrix_weights(k1, k2):
    return pl.pallas_call(
        weights_kernel,
        name="matrix_weights",
        out_shape=[
            jax.ShapeDtypeStruct((3584, 256), BF16),
            jax.ShapeDtypeStruct((4480, 256), BF16),
        ],
        cost_estimate=pl.CostEstimate(flops=0, bytes_accessed=8 << 20, transcendentals=0),
        compiler_params=pltpu.CompilerParams(vmem_limit_bytes=16 << 20),
    )(k1.reshape(49, 32, 64), k2.reshape(49, 64, 128))


def field_kernel(
    acc_ref, r0_ref, r1_ref, m0_ref, m1_ref, f_ref, e_ref, ma_ref, mb_ref, fs, es, et
):
    i = pl.program_id(0)
    last = pl.num_programs(0) - 1
    odd = lax.axis_index("lon") % 2
    upper = lax.axis_index("lat") % 2
    rows = lax.broadcasted_iota(jnp.int32, (32, 128), 0)
    pix = lax.broadcasted_iota(jnp.int32, (32, 128), 1)
    pick = (pix // 4 == (rows % 8) * 4 + rows // 8).astype(F32).astype(BF16)
    keep = (
        lax.broadcasted_iota(jnp.int32, (128, 128), 0) // 32
        == lax.broadcasted_iota(jnp.int32, (128, 128), 1) % 4
    ).astype(F32).astype(BF16)

    is_odd = odd == 1
    for y in range(4):
        east_border = jnp.where(is_odd, r1_ref[0, y], r0_ref[0, y]).astype(F32)
        east_inner = jnp.where(is_odd, r1_ref[1, y], r0_ref[1, y]).astype(F32)
        west_border = jnp.where(is_odd, r0_ref[0, y], r1_ref[0, y]).astype(F32)
        west_inner = jnp.where(is_odd, r0_ref[1, y], r1_ref[1, y]).astype(F32)
        own_east = jnp.where(is_odd, m1_ref[0, y], m0_ref[0, y]).astype(F32)
        own_west = jnp.where(is_odd, m0_ref[0, y], m1_ref[0, y]).astype(F32)
        patches = [acc_ref[y * 8 + c] for c in range(8)]
        patches[0] = patches[0] + west_border
        patches[7] = patches[7] + east_border
        patches = [west_inner + own_west] + patches + [east_inner + own_east]
        for c in range(0, 10, 2):
            pair = [patches[c].astype(BF16), patches[c + 1].astype(BF16)]
            spread = jnp.concatenate(
                [jnp.concatenate([v] * 4, axis=0) * keep for v in pair], axis=0
            )
            both = nt_dot(pick, spread)
            for h in range(2):
                pc = c + h - 1
                for k in range(4):
                    v = both[8 * k : 8 * k + 8, 128 * h : 128 * h + 128]
                    g = 2 * pc + k // 2
                    kk = 4 * pc + k
                    if 0 <= pc < 8:
                        fs[y, k % 2, pl.ds(g, 8, stride=16), :] = v
                    if k % 2 == 0 and 1 <= g <= 16:
                        fs[y, 3, pl.ds(g - 1, 8, stride=16), :] = v
                    if k % 2 == 1 and -1 <= g <= 14:
                        fs[y, 2, pl.ds(g + 1, 8, stride=16), :] = v
                    if kk in (-3, -2, -1, 0, 31, 32, 33):
                        slot = kk + 3 if kk <= 0 else kk - 27
                        e_ref[slot, pl.ds(8 + 32 * i + 8 * y, 8), :] = v
                        et[y, pl.ds(slot, 8, stride=16), :] = v
        for a in range(4):
            f_ref[a, 4 * y : 4 * y + 4] = fs[y, a].astype(BF16).reshape(4, 2, 16, 128)

    @pl.when(i == 0)
    def _():
        for y in range(4):
            et[y, pl.ds(7, 8, stride=16), :] = jnp.zeros((8, 128), F32)
            for z in range(8, 16):
                et[y, pl.ds(z, 8, stride=16), :] = jnp.zeros((8, 128), F32)

    def send(ref, first):
        for a in range(4):
            ref[a] = f_ref[a, first : first + 5]
        for q in range(5):
            y, o = (first + q) // 4, (first + q) % 4
            ref[4, q] = et[y, 32 * o : 32 * o + 32].astype(BF16).reshape(2, 16, 128)

    @pl.when((i == 0) & (upper == 0))
    def _():
        send(ma_ref, 0)

    @pl.when((i == 0) & (upper == 1))
    def _():
        send(mb_ref, 0)

    @pl.when((i == last) & (upper == 0))
    def _():
        send(mb_ref, 11)

    @pl.when((i == last) & (upper == 1))
    def _():
        send(ma_ref, 11)


def build_field(acc, r0, r1, m0, m1):
    four = lambda x: x.reshape(2, 32, 32, 128)
    recv = pl.BlockSpec((2, 4, 32, 128), lambda i: (0, i, 0, 0))
    own = pl.BlockSpec((1, 4, 32, 128), lambda i: (0, i, 0, 0))
    msg = pl.BlockSpec((5, 5, 2, 16, 128), lambda i: (0, 0, 0, 0, 0))
    return pl.pallas_call(
        field_kernel,
        name="build_field",
        grid=(8,),
        in_specs=[pl.BlockSpec((32, 32, 128), lambda i: (i, 0, 0)), recv, recv, own, own],
        out_specs=[
            pl.BlockSpec((4, 16, 2, 16, 128), lambda i: (0, i, 0, 0, 0)),
            pl.BlockSpec((7, 272, 128), lambda i: (0, 0, 0)),
            msg,
            msg,
        ],
        out_shape=[
            jax.ShapeDtypeStruct((4, 128, 2, 16, 128), BF16),
            jax.ShapeDtypeStruct((7, 272, 128), F32),
            jax.ShapeDtypeStruct((5, 5, 2, 16, 128), BF16),
            jax.ShapeDtypeStruct((5, 5, 2, 16, 128), BF16),
        ],
        scratch_shapes=[
            pltpu.VMEM((4, 4, 128, 128), F32),
            pltpu.VMEM((8, 128), F32),
            pltpu.VMEM((4, 128, 128), F32),
        ],
        compiler_params=pltpu.CompilerParams(vmem_limit_bytes=20 << 20),
    )(acc, four(r0), four(r1), four(m0), four(m1))


ORDER = (2, 0, 1, 3)


def first_kernel(f_hbm, e_ref, w_ref, b_ref, g_ref, h_ref, fs, hs, ms, el, ones, sem):
    i = pl.program_id(0)

    def chunk(c):
        return pltpu.make_async_copy(
            f_hbm.at[:, pl.ds(16 * c, 16)], fs.at[:, pl.ds(2 + 16 * c, 16)], sem.at[c]
        )

    def activate(lhs):
        v = jnp.dot(lhs, w_ref[...], preferred_element_type=F32) + b_ref[...]
        return norm_gelu(v, g_ref[...], ones[...], 64)

    @pl.when(i == 0)
    def _():
        for c in range(8):
            chunk(c).start()
        ones[...] = group_ones(256, 64)
        fs[:, 0:2] = jnp.zeros((4, 2, 2, 16, 128), BF16)
        fs[:, 130:132] = jnp.zeros((4, 2, 2, 16, 128), BF16)
        for side in range(2):
            parts = []
            for r in range(7):
                for j in range(4):
                    slot = 4 * side + j
                    if slot == 7:
                        parts.append(jnp.zeros((128, 128), BF16))
                    else:
                        parts.append(e_ref[slot, pl.ds(8 - 3 + r, 128, stride=2), :].astype(BF16))
            el[side] = activate(jnp.concatenate(parts, axis=1))
        chunk(0).wait()

    @pl.when(i < 7)
    def _():
        chunk(jnp.minimum(i + 1, 7)).wait()

    parts = []
    for r in range(7):
        for a in ORDER:
            x = fs[a, pl.ds(16 * i + (r + 1) // 2, 16), (r + 1) % 2]
            parts.append(x.reshape(256, 128))
    h = activate(jnp.concatenate(parts, axis=1))
    for c in range(2):
        hs[c, 8:264] = h[:, 128 * c : 128 * c + 128]
    ms[0] = hs[0, 7:263]
    ms[1] = hs[1, 7:263]
    ms[2] = hs[0, 9:265]
    rows = pl.ds(pl.multiple_of(16 * i, 16), 16)
    ms[0, pl.ds(0, 16, stride=16), :] = el[0, rows, 0:128]
    ms[1, pl.ds(0, 16, stride=16), :] = el[0, rows, 128:256]
    ms[2, pl.ds(15, 16, stride=16), :] = el[1, rows, 0:128]
    tile = lambda v: v.astype(BF16).reshape(8, 2, 16, 128)
    h_ref[0] = tile(ms[0])
    h_ref[1] = tile(ms[1])
    h_ref[2] = tile(hs[0, 8:264])
    h_ref[3] = tile(hs[1, 8:264])
    h_ref[4] = tile(ms[2])


def first_conv(f, e, w1, bias, gain):
    const2 = lambda i: (0, 0)
    return pl.pallas_call(
        first_kernel,
        name="first_conv",
        grid=(8,),
        in_specs=[
            pl.BlockSpec(memory_space=pl.ANY),
            pl.BlockSpec((7, 272, 128), lambda i: (0, 0, 0)),
            pl.BlockSpec((3584, 256), const2),
            pl.BlockSpec((1, 256), const2),
            pl.BlockSpec((1, 256), const2),
        ],
        out_specs=pl.BlockSpec((5, 8, 2, 16, 128), lambda i: (0, i, 0, 0, 0)),
        out_shape=jax.ShapeDtypeStruct((5, 64, 2, 16, 128), BF16),
        scratch_shapes=[
            pltpu.VMEM((4, 132, 2, 16, 128), BF16),
            pltpu.VMEM((2, 272, 128), F32),
            pltpu.VMEM((3, 256, 128), F32),
            pltpu.VMEM((2, 128, 256), F32),
            pltpu.VMEM((256, 256), BF16),
            pltpu.SemaphoreType.DMA((8,)),
        ],
        cost_estimate=pl.CostEstimate(
            flops=2 * 2304 * 3584 * 256, bytes_accessed=12 << 20, transcendentals=1 << 20
        ),
        compiler_params=pltpu.CompilerParams(vmem_limit_bytes=28 << 20),
    )(f, e, w1, bias, gain)


BASES = (0, 2, 4, 11, 13, 20, 27, 29)


def second_kernel(
    h_hbm, ma_ref, mb_ref, ra_ref, rb_ref, w1_ref, w2_hbm, b1_ref, g1_ref, b2_ref, g2_ref,
    o_ref, hs, w2, ve, vf, le, ts, ms, os, ones1, ones2, sem,
):
    i = pl.program_id(0)
    lat = lax.axis_index("lat")
    odd = lat % 2 == 1
    north = lat == 0
    south = lat == 3

    @pl.when(i == 0)
    def _():
        body = pltpu.make_async_copy(h_hbm, hs.at[:, 2:66], sem.at[0])
        body.start()
        weights = pltpu.make_async_copy(w2_hbm, w2, sem.at[1])
        weights.start()
        ones1[...] = group_ones(256, 64)
        ones2[...] = group_ones(256, 128)

        def row(ref, a, m):
            return ref[a, m // 2, m % 2]

        def own_top(a, m):
            return jnp.where(odd, row(mb_ref, a, m), row(ma_ref, a, m))

        def own_bot(a, m):
            return jnp.where(odd, row(ma_ref, a, m), row(mb_ref, a, m))

        def halo_top(a, m):
            return jnp.where(odd, row(rb_ref, a, m), row(ra_ref, a, m))

        def halo_bot(a, m):
            return jnp.where(odd, row(ra_ref, a, m), row(rb_ref, a, m))

        for a in range(5):
            def put(n, v):
                if a < 4:
                    vf[a, n] = v
                else:
                    ve[16 * n : 16 * n + 16] = v.astype(F32)

            for q in range(11):
                normal = halo_top(a, q + 1) if q < 9 else own_top(a, q - 9)
                polar = own_top(a, 2 - q) if q < 3 else halo_top(a, q - 3)
                put(q, jnp.where(north, polar, normal))
            for q in range(9):
                if q < 3:
                    v = jnp.where(north, halo_top(a, 2 - q), halo_top(a, 7 + q))
                else:
                    v = own_top(a, q - 3)
                put(11 + q, v)
            for q in range(7):
                if q < 5:
                    v = own_bot(a, 5 + q)
                else:
                    v = jnp.where(south, halo_bot(a, 14 - q), halo_bot(a, q - 5))
                put(20 + q, v)
            for q in range(9):
                normal = own_bot(a, 7 + q) if q < 3 else halo_bot(a, q - 3)
                polar = halo_bot(a, 3 + q) if q < 7 else own_bot(a, 16 - q)
                put(27 + q, jnp.where(south, polar, normal))

        for n, base in enumerate(BASES):
            for r in range(7):
                for j in range(4):
                    col = 128 * (4 * r + j)
                    for side in range(2):
                        src = 16 * (base + r) + 4 * side + j
                        le[n + 8 * side : n + 8 * side + 1, col : col + 128] = ve[src : src + 1, :]
        parts = []
        for r in range(7):
            for a in ORDER:
                parts.append(jnp.concatenate([vf[a, base + r] for base in BASES], axis=0))
        lhs = jnp.concatenate([jnp.concatenate(parts, axis=1), le[...].astype(BF16)], axis=0)
        v = jnp.dot(lhs, w1_ref[...], preferred_element_type=F32) + b1_ref[...]
        h = norm_gelu(v, g1_ref[...], ones1[...], 64)
        for c in range(2):
            ts[c, 8:136] = h[0:128, 128 * c : 128 * c + 128]
        ms[0] = ts[0, 7:135]
        ms[1] = ts[1, 7:135]
        ms[2] = ts[0, 9:137]
        ms[0, pl.ds(0, 8, stride=16), :] = h[128:136, 0:128]
        ms[1, pl.ds(0, 8, stride=16), :] = h[128:136, 128:256]
        ms[2, pl.ds(15, 8, stride=16), :] = h[136:144, 0:128]
        body.wait()
        full = [ms[0], ms[1], ts[0, 8:136], ts[1, 8:136], ms[2]]
        for a in range(5):
            v = full[a].astype(BF16).reshape(8, 16, 128)
            for n in range(3):
                to = jnp.where(north, 3 - n, 1 + n)
                hs[a, to // 2, to % 2] = v[n]
            hs[a, 2, 0] = v[3]
            hs[a, 2, 1] = v[4]
            hs[a, 65, 1] = v[5]
            for n in range(2):
                to = jnp.where(south, 1 - n, n)
                hs[a, 66, to] = v[6 + n]
        weights.wait()

    parts = []
    for r in range(7):
        for a in range(5):
            x = hs[a, pl.ds(16 * i + (r + 1) // 2, 16), (r + 1) % 2]
            parts.append(x.reshape(256, 128))
    v = jnp.dot(jnp.concatenate(parts, axis=1), w2[...], preferred_element_type=F32) + b2_ref[...]
    y = norm_gelu(v, g2_ref[...], ones2[...], 128)
    for t in range(2):
        os[pl.ds(t, 256, stride=2), :] = y[:, 128 * t : 128 * t + 128]
    o_ref[...] = os[...].astype(BF16).reshape(16, 32, 128)


def second_conv(h, ma, mb, ra, rb, w1, w2, b1, g1, b2, g2):
    const2 = lambda i: (0, 0)
    msg = pl.BlockSpec((5, 5, 2, 16, 128), lambda i: (0, 0, 0, 0, 0))
    vec = pl.BlockSpec((1, 256), const2)
    return pl.pallas_call(
        second_kernel,
        name="second_conv",
        grid=(4,),
        in_specs=[
            pl.BlockSpec(memory_space=pl.ANY),
            msg,
            msg,
            msg,
            msg,
            pl.BlockSpec((3584, 256), const2),
            pl.BlockSpec(memory_space=pl.ANY),
            vec,
            vec,
            vec,
            vec,
        ],
        out_specs=pl.BlockSpec((16, 32, 128), lambda i: (i, 0, 0)),
        out_shape=jax.ShapeDtypeStruct((64, 32, 128), BF16),
        scratch_shapes=[
            pltpu.VMEM((5, 68, 2, 16, 128), BF16),
            pltpu.VMEM((4480, 256), BF16),
            pltpu.VMEM((36 * 16, 128), F32),
            pltpu.VMEM((4, 36, 16, 128), BF16),
            pltpu.VMEM((16, 3584), F32),
            pltpu.VMEM((2, 144, 128), F32),
            pltpu.VMEM((3, 128, 128), F32),
            pltpu.VMEM((512, 128), F32),
            pltpu.VMEM((256, 256), BF16),
            pltpu.VMEM((256, 256), BF16),
            pltpu.SemaphoreType.DMA((2,)),
        ],
        compiler_params=pltpu.CompilerParams(vmem_limit_bytes=28 << 20),
    )(h, ma, mb, ra, rb, w1, w2, b1, g1, b2, g2)


def local(
    cell_state,
    remap_weight,
    block_target,
    block_count,
    border_state,
    border_weight,
    border_target,
    kernel_one,
    bias_one,
    gain_one,
    kernel_two,
    bias_two,
    gain_two,
):
    acc, m0, m1 = block_sums(
        block_target[0, 0],
        block_count[0],
        border_target[0, 0],
        border_state[0, 0],
        border_weight[0, 0],
        cell_state[0, 0],
        remap_weight[0, 0],
    )
    r0 = exchange(m0, LON_EVEN)
    r1 = exchange(m1, LON_ODD)
    w1, w2 = matrix_weights(kernel_one, kernel_two)
    f, e, ma, mb = build_field(acc, r0, r1, m0, m1)
    ra = exchange(ma, LAT_OUTER)
    rb = exchange(mb, LAT_INNER)
    b1 = jnp.tile(bias_one, 4)[None]
    g1 = jnp.tile(gain_one, 4)[None]
    b2 = jnp.tile(bias_two, 2)[None]
    g2 = jnp.tile(gain_two, 2)[None]
    h = first_conv(f, e, w1, b1, g1)
    return second_conv(h, ma, mb, ra, rb, w1, w2, b1, g1, b2, g2)


def solution(mesh):
    placed = (
        P("lat", "lon", None, None, None),
        P("lat", "lon", None, None, None),
        P("lat", "lon", None),
        P("lat", "lon"),
        P("lat", "lon", None, None, None),
        P("lat", "lon", None, None, None),
        P("lat", "lon", None),
        P(),
        P(),
        P(),
        P(),
        P(),
        P(),
    )
    return jax.shard_map(
        local, mesh=mesh, in_specs=placed, out_specs=P("lat", "lon", None), check_vma=False
    )
```

```python
import jax
import jax.numpy as jnp
from jax import lax
from jax.experimental import pallas as pl
from jax.experimental.pallas import tpu as pltpu
from jax.sharding import PartitionSpec as P

F32 = jnp.float32
BF16 = jnp.bfloat16
BANDS = 4
SECTORS = 32
BIG = 24 << 20


def mesh_pairs(partner):
    return [
        (b * SECTORS + s, (lambda t: t[0] * SECTORS + t[1] % SECTORS)(partner(b, s)))
        for b in range(BANDS)
        for s in range(SECTORS)
    ]


LON_EVEN = mesh_pairs(lambda b, s: (b, s ^ 1))
LON_ODD = mesh_pairs(lambda b, s: (b, s + 1 if s % 2 else s - 1))
LAT_OUTER = mesh_pairs(
    lambda b, s: {0: (0, s + 16), 1: (2, s), 2: (1, s), 3: (3, s + 16)}[b]
)
LAT_INNER = mesh_pairs(lambda b, s: (b ^ 1, s))


def exchange(block, pairs):
    return lax.ppermute(block, ("lat", "lon"), pairs)


def nt_dot(a, b):
    return lax.dot_general(a, b, (((1,), (1,)), ((), ())), preferred_element_type=F32)


def group_ones(size, width):
    rows = lax.broadcasted_iota(jnp.int32, (size, size), 0) // width
    cols = lax.broadcasted_iota(jnp.int32, (size, size), 1) // width
    return (rows == cols).astype(F32).astype(BF16)


def norm_gelu(v, gain, ones, width):
    sq = v * v
    hi = sq.astype(BF16)
    lo = (sq - hi.astype(F32)).astype(BF16)
    total = jnp.dot(hi, ones, preferred_element_type=F32)
    total = total + jnp.dot(lo, ones, preferred_element_type=F32)
    x = v * lax.rsqrt(total * (1.0 / width) + 1e-05) * gain
    return jax.nn.gelu(x, approximate=True)


def unit(size):
    rows = lax.broadcasted_iota(jnp.int32, (size, size), 0)
    cols = lax.broadcasted_iota(jnp.int32, (size, size), 1)
    return (rows == cols).astype(F32).astype(BF16)


HBM = pl.BlockSpec(memory_space=pltpu.HBM)
SMEM = pl.BlockSpec(memory_space=pltpu.SMEM)
VMEM = pl.BlockSpec(memory_space=pltpu.VMEM)


def in_hbm(x):
    return pltpu.with_memory_space_constraint(x, pltpu.HBM)


def half_lanes():
    lanes = lax.broadcasted_iota(jnp.int32, (16, 128), 1)
    low = (lanes < 64).astype(F32).astype(BF16)
    high = (lanes >= 64).astype(F32).astype(BF16)
    return low, high


def send_sides(m0_ref, m1_ref, east, west):
    odd = lax.axis_index("lon") % 2

    def fill(east_ref, west_ref):
        for q in range(32):
            east_ref[q] = east(q).astype(BF16)
            west_ref[q] = west(q).astype(BF16)

    @pl.when(odd == 0)
    def _():
        fill(m0_ref, m1_ref)

    @pl.when(odd == 1)
    def _():
        fill(m1_ref, m0_ref)


def border_kernel(btarget, x_hbm, w_hbm, m0_ref, m1_ref, token, xv, wv, st, sb, acc, sem):
    states = pltpu.make_async_copy(x_hbm, xv, sem.at[4])
    states.start()
    chunks = [
        pltpu.make_async_copy(
            w_hbm.at[pl.ds(32 * c, 32)], wv.at[pl.ds(32 * c, 32)], sem.at[c]
        )
        for c in range(4)
    ]
    for c in chunks:
        c.start()
    acc[...] = jnp.zeros_like(acc)
    low, high = half_lanes()
    eye = unit(128)
    states.wait()
    for c in range(0, 16, 2):
        x = jnp.concatenate([xv[c], xv[c + 16], xv[c + 1], xv[c + 17]], axis=0)
        out = nt_dot(eye, x)
        st[pl.ds(c, 128, stride=16), :] = out[:, :128]
        st[pl.ds(c + 1, 128, stride=16), :] = out[:, 128:]
    for q in range(8):
        sb[16 * q : 16 * q + 16] = st[256 * q : 256 * q + 256].astype(BF16).reshape(16, 16, 128)
    for c in range(4):
        chunks[c].wait()

        def body(carry, c=c):
            n0 = 32 * c
            vals = []
            for u in range(0, 32, 2):
                rows = [sb[n0 + u + k] * half for k in range(2) for half in (low, high)]
                w = jnp.concatenate([wv[n0 + u], wv[n0 + u + 1]], axis=1)
                rhs = jnp.concatenate([w, w], axis=0)
                vals.append(
                    jnp.dot(jnp.concatenate(rows, axis=0), rhs, preferred_element_type=F32)
                )
            for u in range(32):
                k = u % 2
                acc[btarget[n0 + u]] += vals[u // 2][32 * k : 32 * k + 32, 128 * k : 128 * k + 128]
            return carry

        body(0)
    send_sides(m0_ref, m1_ref, lambda q: acc[32 + q], lambda q: acc[q])
    token[...] = jnp.zeros_like(token)


def border_sums(btarget, bstate, bweight):
    side = jax.ShapeDtypeStruct((32, 32, 128), BF16)
    return pl.pallas_call(
        border_kernel,
        name="border_sums",
        in_specs=[SMEM, HBM, HBM],
        out_specs=[VMEM, VMEM, VMEM],
        out_shape=[side, side, jax.ShapeDtypeStruct((8, 128), F32)],
        scratch_shapes=[
            pltpu.VMEM((32, 64, 128), BF16),
            pltpu.VMEM((128, 64, 128), BF16),
            pltpu.VMEM((2048, 128), F32),
            pltpu.VMEM((128, 16, 128), BF16),
            pltpu.VMEM((64, 32, 128), F32),
            pltpu.SemaphoreType.DMA((5,)),
        ],
        cost_estimate=pl.CostEstimate(
            flops=2 * 128 * 32 * 64 * 128, bytes_accessed=4 << 20, transcendentals=0
        ),
        compiler_params=pltpu.CompilerParams(vmem_limit_bytes=BIG),
    )(btarget, in_hbm(jnp.transpose(bstate, (1, 2, 0))), in_hbm(bweight))


def sums_kernel(
    target, count, after, x_hbm, w_hbm, acc_ref, m0_ref, m1_ref, xv, wv, st, sb, xsem, wsem
):
    states = [
        pltpu.make_async_copy(x_hbm.at[:, :, pl.ds(256 * p, 256)], xv.at[p], xsem.at[p])
        for p in range(2)
    ]
    chunks = {
        (p, c, h): pltpu.make_async_copy(
            w_hbm.at[pl.ds(256 * p + 128 * h + 32 * c, 32)],
            wv.at[pl.ds(256 * p + 128 * h + 32 * c, 32)],
            wsem.at[p, c, h],
        )
        for p in range(2)
        for c in range(4)
        for h in range(2)
    }
    for p in range(2):
        states[p].start()
        for c in range(4):
            for h in range(2):
                chunks[p, c, h].start()
    low, high = half_lanes()
    low = jnp.concatenate([low, low], axis=0)
    high = jnp.concatenate([high, high], axis=0)
    eye = unit(128)
    for p in range(2):
        states[p].wait()
        for c in range(0, 32, 2):
            x = jnp.concatenate(
                [xv[p, c + k, :, 128 * h : 128 * h + 128] for k in range(2) for h in range(2)], axis=0
            )
            out = nt_dot(eye, x)
            st[pl.ds(c, 128, stride=32), :] = out[:, :128]
            st[pl.ds(c + 1, 128, stride=32), :] = out[:, 128:]
        for q in range(16):
            sb[8 * q : 8 * q + 8] = st[256 * q : 256 * q + 256].astype(BF16).reshape(8, 32, 128)
        for c in range(4):
            chunks[p, c, 0].wait()
            chunks[p, c, 1].wait()

            n0 = 32 * c
            for u in range(0, 32, 2):
                rows = [sb[n0 + u + k] * half for k in range(2) for half in (low, high)]
                cols = [
                    [wv[256 * p + 128 * h + n0 + u + k] for k in range(2)] for h in range(2)
                ]
                rhs = jnp.concatenate([jnp.concatenate(r, axis=1) for r in cols], axis=0)
                both = jnp.dot(jnp.concatenate(rows, axis=0), rhs, preferred_element_type=F32)
                for k in range(2):
                    for h in range(2):
                        n = 256 * p + 128 * h + n0 + u + k
                        at = 64 * k + 32 * h
                        v = both[at : at + 32, 128 * k : 128 * k + 128]
                        if p == 0:
                            acc_ref[target[n]] = v
                        else:
                            acc_ref[jnp.where(n < count[0], target[n], 256)] += v
    send_sides(m0_ref, m1_ref, lambda q: acc_ref[8 * q + 7], lambda q: acc_ref[8 * q])


def inner_sums(target, count, after, state, weight):
    side = jax.ShapeDtypeStruct((32, 32, 128), BF16)
    return pl.pallas_call(
        sums_kernel,
        name="inner_sums",
        in_specs=[SMEM, SMEM, VMEM, HBM, HBM],
        out_specs=[VMEM, VMEM, VMEM],
        out_shape=[pltpu.VMEM((257, 32, 128), F32), side, side],
        scratch_shapes=[
            pltpu.VMEM((2, 32, 64, 256), BF16),
            pltpu.VMEM((512, 64, 128), BF16),
            pltpu.VMEM((4096, 128), F32),
            pltpu.VMEM((128, 32, 128), BF16),
            pltpu.SemaphoreType.DMA((2,)),
            pltpu.SemaphoreType.DMA((2, 4, 2)),
        ],
        cost_estimate=pl.CostEstimate(
            flops=2 * 512 * 32 * 64 * 128, bytes_accessed=16 << 20, transcendentals=0
        ),
        compiler_params=pltpu.CompilerParams(vmem_limit_bytes=BIG),
    )(target, count, after, in_hbm(jnp.transpose(state, (1, 2, 0))), in_hbm(weight))


def weights_kernel(k1_ref, k2_ref, b1_ref, g1_ref, b2_ref, g2_ref, w1_ref, w2_ref, v_ref):
    w1_ref[...] = jnp.zeros_like(w1_ref)
    w2_ref[...] = jnp.zeros_like(w2_ref)
    for r in range(7):
        for s in range(7):
            for t in range(4):
                row = r * 512 + (2 * t + s + 1) * 32
                w1_ref[row : row + 32, t * 64 : (t + 1) * 64] = k1_ref[r * 7 + s]
            for t in range(2):
                row = r * 640 + (2 * t + s + 1) * 64
                w2_ref[row : row + 64, t * 128 : (t + 1) * 128] = k2_ref[r * 7 + s]
    for t in range(4):
        v_ref[0:1, t * 64 : (t + 1) * 64] = b1_ref[...]
        v_ref[1:2, t * 64 : (t + 1) * 64] = g1_ref[...]
    for t in range(2):
        v_ref[2:3, t * 128 : (t + 1) * 128] = b2_ref[...]
        v_ref[3:4, t * 128 : (t + 1) * 128] = g2_ref[...]


def matrix_weights(k1, k2, b1, g1, b2, g2):
    return pl.pallas_call(
        weights_kernel,
        name="matrix_weights",
        out_shape=[
            jax.ShapeDtypeStruct((3584, 256), BF16),
            jax.ShapeDtypeStruct((4480, 256), BF16),
            jax.ShapeDtypeStruct((8, 256), F32),
        ],
        cost_estimate=pl.CostEstimate(flops=0, bytes_accessed=8 << 20, transcendentals=0),
        compiler_params=pltpu.CompilerParams(vmem_limit_bytes=16 << 20),
    )(k1.reshape(49, 32, 64), k2.reshape(49, 64, 128), b1[None], g1[None], b2[None], g2[None])


def field_kernel(
    acc, rb0_ref, rb1_ref, ri0_ref, ri1_ref, m0_ref, m1_ref, f_ref, e_ref, ma_ref, mb_ref, fs, et
):
    i = pl.program_id(0)
    last = pl.num_programs(0) - 1
    odd = lax.axis_index("lon") % 2
    upper = lax.axis_index("lat") % 2
    rows = lax.broadcasted_iota(jnp.int32, (32, 128), 0)
    pix = lax.broadcasted_iota(jnp.int32, (32, 128), 1)
    pick = (pix // 4 == (rows % 8) * 4 + rows // 8).astype(F32).astype(BF16)
    keep = (
        lax.broadcasted_iota(jnp.int32, (128, 128), 0) // 32
        == lax.broadcasted_iota(jnp.int32, (128, 128), 1) % 4
    ).astype(F32).astype(BF16)

    is_odd = odd == 1
    for y in range(4):
        east_border = jnp.where(is_odd, rb1_ref[y], rb0_ref[y]).astype(F32)
        east_inner = jnp.where(is_odd, ri1_ref[y], ri0_ref[y]).astype(F32)
        west_border = jnp.where(is_odd, rb0_ref[y], rb1_ref[y]).astype(F32)
        west_inner = jnp.where(is_odd, ri0_ref[y], ri1_ref[y]).astype(F32)
        own_east = jnp.where(is_odd, m1_ref[y], m0_ref[y]).astype(F32)
        own_west = jnp.where(is_odd, m0_ref[y], m1_ref[y]).astype(F32)
        patches = [acc[32 * i + 8 * y + c] for c in range(8)]
        patches[0] = patches[0] + west_border
        patches[7] = patches[7] + east_border
        patches = [west_inner + own_west] + patches + [east_inner + own_east]
        for c in range(0, 10, 2):
            pair = [patches[c].astype(BF16), patches[c + 1].astype(BF16)]
            spread = jnp.concatenate(
                [jnp.concatenate([v] * 4, axis=0) * keep for v in pair], axis=0
            )
            both = nt_dot(pick, spread)
            for h in range(2):
                pc = c + h - 1
                for k in range(4):
                    v = both[8 * k : 8 * k + 8, 128 * h : 128 * h + 128]
                    g = 2 * pc + k // 2
                    kk = 4 * pc + k
                    if 0 <= pc < 8:
                        fs[y, k % 2, pl.ds(g, 8, stride=16), :] = v
                    if k % 2 == 0 and 1 <= g <= 16:
                        fs[y, 3, pl.ds(g - 1, 8, stride=16), :] = v
                    if k % 2 == 1 and -1 <= g <= 14:
                        fs[y, 2, pl.ds(g + 1, 8, stride=16), :] = v
                    if kk in (-3, -2, -1, 0, 31, 32, 33):
                        slot = kk + 3 if kk <= 0 else kk - 27
                        e_ref[slot, pl.ds(8 + 32 * i + 8 * y, 8), :] = v
                        et[y, pl.ds(slot, 8, stride=16), :] = v
        for a in range(4):
            f_ref[a, 4 * y : 4 * y + 4] = fs[y, a].astype(BF16).reshape(4, 2, 16, 128)

    @pl.when(i == 0)
    def _():
        for y in range(4):
            et[y, pl.ds(7, 8, stride=16), :] = jnp.zeros((8, 128), F32)
            for z in range(8, 16):
                et[y, pl.ds(z, 8, stride=16), :] = jnp.zeros((8, 128), F32)

    def send(ref, first):
        for a in range(4):
            ref[a] = f_ref[a, first : first + 5]
        for q in range(5):
            y, o = (first + q) // 4, (first + q) % 4
            ref[4, q] = et[y, 32 * o : 32 * o + 32].astype(BF16).reshape(2, 16, 128)

    @pl.when((i == 0) & (upper == 0))
    def _():
        send(ma_ref, 0)

    @pl.when((i == 0) & (upper == 1))
    def _():
        send(mb_ref, 0)

    @pl.when((i == last) & (upper == 0))
    def _():
        send(mb_ref, 11)

    @pl.when((i == last) & (upper == 1))
    def _():
        send(ma_ref, 11)


def build_field(acc, *sides):
    side = pl.BlockSpec((4, 32, 128), lambda i: (i, 0, 0))
    msg = pl.BlockSpec((5, 5, 2, 16, 128), lambda i: (0, 0, 0, 0, 0))
    return pl.pallas_call(
        field_kernel,
        name="build_field",
        grid=(8,),
        in_specs=[VMEM] + [side] * 6,
        out_specs=[
            pl.BlockSpec((4, 16, 2, 16, 128), lambda i: (0, i, 0, 0, 0)),
            pl.BlockSpec((7, 272, 128), lambda i: (0, 0, 0)),
            msg,
            msg,
        ],
        out_shape=[
            jax.ShapeDtypeStruct((4, 128, 2, 16, 128), BF16),
            jax.ShapeDtypeStruct((7, 272, 128), F32),
            jax.ShapeDtypeStruct((5, 5, 2, 16, 128), BF16),
            jax.ShapeDtypeStruct((5, 5, 2, 16, 128), BF16),
        ],
        scratch_shapes=[
            pltpu.VMEM((4, 4, 128, 128), F32),
            pltpu.VMEM((4, 128, 128), F32),
        ],
        compiler_params=pltpu.CompilerParams(vmem_limit_bytes=24 << 20),
    )(acc, *sides)


ORDER = (2, 0, 1, 3)


def first_kernel(f_hbm, e_ref, w_ref, v_ref, h_ref, fs, hs, ms, el, ones, sem):
    i = pl.program_id(0)

    def chunk(c):
        return pltpu.make_async_copy(
            f_hbm.at[:, pl.ds(16 * c, 16)], fs.at[:, pl.ds(2 + 16 * c, 16)], sem.at[c]
        )

    def activate(lhs):
        v = jnp.dot(lhs, w_ref[...], preferred_element_type=F32) + v_ref[0:1]
        return norm_gelu(v, v_ref[1:2], ones[...], 64)

    @pl.when(i == 0)
    def _():
        for c in range(8):
            chunk(c).start()
        ones[...] = group_ones(256, 64)
        fs[:, 0:2] = jnp.zeros((4, 2, 2, 16, 128), BF16)
        fs[:, 130:132] = jnp.zeros((4, 2, 2, 16, 128), BF16)
        for side in range(2):
            parts = []
            for r in range(7):
                for j in range(4):
                    slot = 4 * side + j
                    if slot == 7:
                        parts.append(jnp.zeros((128, 128), BF16))
                    else:
                        parts.append(e_ref[slot, pl.ds(8 - 3 + r, 128, stride=2), :].astype(BF16))
            el[side] = activate(jnp.concatenate(parts, axis=1))
        chunk(0).wait()

    for z in range(4):

        @pl.when(4 * i + z < 7)
        def _():
            chunk(jnp.minimum(4 * i + z + 1, 7)).wait()


    parts = []
    for r in range(7):
        for a in ORDER:
            x = fs[a, pl.ds(64 * i + (r + 1) // 2, 64), (r + 1) % 2]
            parts.append(x.reshape(1024, 128))
    h = activate(jnp.concatenate(parts, axis=1))
    for c in range(2):
        hs[c, 8:1032] = h[:, 128 * c : 128 * c + 128]
    ms[0] = hs[0, 7:1031]
    ms[1] = hs[1, 7:1031]
    ms[2] = hs[0, 9:1033]
    rows = pl.ds(pl.multiple_of(64 * i, 64), 64)
    ms[0, pl.ds(0, 64, stride=16), :] = el[0, rows, 0:128]
    ms[1, pl.ds(0, 64, stride=16), :] = el[0, rows, 128:256]
    ms[2, pl.ds(15, 64, stride=16), :] = el[1, rows, 0:128]
    tile = lambda v: v.astype(BF16).reshape(32, 2, 16, 128)
    h_ref[0] = tile(ms[0])
    h_ref[1] = tile(ms[1])
    h_ref[2] = tile(hs[0, 8:1032])
    h_ref[3] = tile(hs[1, 8:1032])
    h_ref[4] = tile(ms[2])


def first_conv(f, e, w1, vec):
    const2 = lambda i: (0, 0)
    return pl.pallas_call(
        first_kernel,
        name="first_conv",
        grid=(2,),
        in_specs=[
            pl.BlockSpec(memory_space=pl.ANY),
            pl.BlockSpec((7, 272, 128), lambda i: (0, 0, 0)),
            pl.BlockSpec((3584, 256), const2),
            pl.BlockSpec((8, 256), const2),
        ],
        out_specs=pl.BlockSpec((5, 32, 2, 16, 128), lambda i: (0, i, 0, 0, 0)),
        out_shape=jax.ShapeDtypeStruct((5, 64, 2, 16, 128), BF16),
        scratch_shapes=[
            pltpu.VMEM((4, 132, 2, 16, 128), BF16),
            pltpu.VMEM((2, 1040, 128), F32),
            pltpu.VMEM((3, 1024, 128), F32),
            pltpu.VMEM((2, 128, 256), F32),
            pltpu.VMEM((256, 256), BF16),
            pltpu.SemaphoreType.DMA((8,)),
        ],
        cost_estimate=pl.CostEstimate(
            flops=2 * 2304 * 3584 * 256, bytes_accessed=12 << 20, transcendentals=1 << 20
        ),
        compiler_params=pltpu.CompilerParams(vmem_limit_bytes=28 << 20),
    )(f, e, w1, vec)


BASES = (0, 2, 4, 11, 13, 20, 27, 29)


def second_kernel(
    h_hbm, ma_ref, mb_ref, ra_ref, rb_ref, w1_ref, w2_hbm, v_ref,
    o_ref, hs, w2, ve, vf, le, ts, ms, os, ones1, ones2, sem,
):
    i = pl.program_id(0)
    lat = lax.axis_index("lat")
    odd = lat % 2 == 1
    north = lat == 0
    south = lat == 3

    @pl.when(i == 0)
    def _():
        body = pltpu.make_async_copy(h_hbm, hs.at[:, 2:66], sem.at[0])
        body.start()
        weights = pltpu.make_async_copy(w2_hbm, w2, sem.at[1])
        weights.start()
        ones1[...] = group_ones(256, 64)
        ones2[...] = group_ones(256, 128)

        def row(ref, a, m):
            return ref[a, m // 2, m % 2]

        def own_top(a, m):
            return jnp.where(odd, row(mb_ref, a, m), row(ma_ref, a, m))

        def own_bot(a, m):
            return jnp.where(odd, row(ma_ref, a, m), row(mb_ref, a, m))

        def halo_top(a, m):
            return jnp.where(odd, row(rb_ref, a, m), row(ra_ref, a, m))

        def halo_bot(a, m):
            return jnp.where(odd, row(ra_ref, a, m), row(rb_ref, a, m))

        for a in range(5):
            def put(n, v):
                if a < 4:
                    vf[a, n] = v
                else:
                    ve[16 * n : 16 * n + 16] = v.astype(F32)

            for q in range(11):
                normal = halo_top(a, q + 1) if q < 9 else own_top(a, q - 9)
                polar = own_top(a, 2 - q) if q < 3 else halo_top(a, q - 3)
                put(q, jnp.where(north, polar, normal))
            for q in range(9):
                if q < 3:
                    v = jnp.where(north, halo_top(a, 2 - q), halo_top(a, 7 + q))
                else:
                    v = own_top(a, q - 3)
                put(11 + q, v)
            for q in range(7):
                if q < 5:
                    v = own_bot(a, 5 + q)
                else:
                    v = jnp.where(south, halo_bot(a, 14 - q), halo_bot(a, q - 5))
                put(20 + q, v)
            for q in range(9):
                normal = own_bot(a, 7 + q) if q < 3 else halo_bot(a, q - 3)
                polar = halo_bot(a, 3 + q) if q < 7 else own_bot(a, 16 - q)
                put(27 + q, jnp.where(south, polar, normal))

        for n, base in enumerate(BASES):
            for r in range(7):
                for j in range(4):
                    col = 128 * (4 * r + j)
                    for side in range(2):
                        src = 16 * (base + r) + 4 * side + j
                        le[n + 8 * side : n + 8 * side + 1, col : col + 128] = ve[src : src + 1, :]
        parts = []
        for r in range(7):
            for a in ORDER:
                parts.append(jnp.concatenate([vf[a, base + r] for base in BASES], axis=0))
        lhs = jnp.concatenate([jnp.concatenate(parts, axis=1), le[...].astype(BF16)], axis=0)
        v = jnp.dot(lhs, w1_ref[...], preferred_element_type=F32) + v_ref[0:1]
        h = norm_gelu(v, v_ref[1:2], ones1[...], 64)
        for c in range(2):
            ts[c, 8:136] = h[0:128, 128 * c : 128 * c + 128]
        ms[0] = ts[0, 7:135]
        ms[1] = ts[1, 7:135]
        ms[2] = ts[0, 9:137]
        ms[0, pl.ds(0, 8, stride=16), :] = h[128:136, 0:128]
        ms[1, pl.ds(0, 8, stride=16), :] = h[128:136, 128:256]
        ms[2, pl.ds(15, 8, stride=16), :] = h[136:144, 0:128]
        body.wait()
        full = [ms[0], ms[1], ts[0, 8:136], ts[1, 8:136], ms[2]]
        for a in range(5):
            v = full[a].astype(BF16).reshape(8, 16, 128)
            for n in range(3):
                to = jnp.where(north, 3 - n, 1 + n)
                hs[a, to // 2, to % 2] = v[n]
            hs[a, 2, 0] = v[3]
            hs[a, 2, 1] = v[4]
            hs[a, 65, 1] = v[5]
            for n in range(2):
                to = jnp.where(south, 1 - n, n)
                hs[a, 66, to] = v[6 + n]
        weights.wait()

    parts = []
    for r in range(7):
        for a in range(5):
            x = hs[a, pl.ds(16 * i + (r + 1) // 2, 16), (r + 1) % 2]
            parts.append(x.reshape(256, 128))
    v = jnp.dot(jnp.concatenate(parts, axis=1), w2[...], preferred_element_type=F32) + v_ref[2:3]
    y = norm_gelu(v, v_ref[3:4], ones2[...], 128)
    for t in range(2):
        os[pl.ds(t, 256, stride=2), :] = y[:, 128 * t : 128 * t + 128]
    o_ref[...] = os[...].astype(BF16).reshape(16, 32, 128)


def second_conv(h, ma, mb, ra, rb, w1, w2, vec):
    const2 = lambda i: (0, 0)
    msg = pl.BlockSpec((5, 5, 2, 16, 128), lambda i: (0, 0, 0, 0, 0))
    return pl.pallas_call(
        second_kernel,
        name="second_conv",
        grid=(4,),
        in_specs=[
            pl.BlockSpec(memory_space=pl.ANY),
            msg,
            msg,
            msg,
            msg,
            pl.BlockSpec((3584, 256), const2),
            pl.BlockSpec(memory_space=pl.ANY),
            pl.BlockSpec((8, 256), const2),
        ],
        out_specs=pl.BlockSpec((16, 32, 128), lambda i: (i, 0, 0)),
        out_shape=jax.ShapeDtypeStruct((64, 32, 128), BF16),
        scratch_shapes=[
            pltpu.VMEM((5, 68, 2, 16, 128), BF16),
            pltpu.VMEM((4480, 256), BF16),
            pltpu.VMEM((36 * 16, 128), F32),
            pltpu.VMEM((4, 36, 16, 128), BF16),
            pltpu.VMEM((16, 3584), F32),
            pltpu.VMEM((2, 144, 128), F32),
            pltpu.VMEM((3, 128, 128), F32),
            pltpu.VMEM((512, 128), F32),
            pltpu.VMEM((256, 256), BF16),
            pltpu.VMEM((256, 256), BF16),
            pltpu.SemaphoreType.DMA((2,)),
        ],
        compiler_params=pltpu.CompilerParams(vmem_limit_bytes=28 << 20),
    )(h, ma, mb, ra, rb, w1, w2, vec)


def local(
    cell_state,
    remap_weight,
    block_target,
    block_count,
    border_state,
    border_weight,
    border_target,
    kernel_one,
    bias_one,
    gain_one,
    kernel_two,
    bias_two,
    gain_two,
):
    m0, m1, after = border_sums(border_target[0, 0], border_state[0, 0], border_weight[0, 0])
    rb0 = exchange(m0, LON_EVEN)
    rb1 = exchange(m1, LON_ODD)
    acc, i0, i1 = inner_sums(
        block_target[0, 0], block_count[0], after, cell_state[0, 0], remap_weight[0, 0]
    )
    ri0 = exchange(i0, LON_EVEN)
    ri1 = exchange(i1, LON_ODD)
    w1, w2, vec = matrix_weights(kernel_one, kernel_two, bias_one, gain_one, bias_two, gain_two)
    f, e, ma, mb = build_field(acc, rb0, rb1, ri0, ri1, m0, m1)
    ra = exchange(ma, LAT_OUTER)
    rb = exchange(mb, LAT_INNER)
    h = first_conv(f, e, w1, vec)
    return second_conv(h, ma, mb, ra, rb, w1, w2, vec)


def solution(mesh):
    placed = (
        P("lat", "lon", None, None, None),
        P("lat", "lon", None, None, None),
        P("lat", "lon", None),
        P("lat", "lon"),
        P("lat", "lon", None, None, None),
        P("lat", "lon", None, None, None),
        P("lat", "lon", None),
        P(),
        P(),
        P(),
        P(),
        P(),
        P(),
    )
    return jax.shard_map(
        local, mesh=mesh, in_specs=placed, out_specs=P("lat", "lon", None), check_vma=False
    )
```

```python
import jax
import jax.numpy as jnp
from jax import lax
from jax.experimental import pallas as pl
from jax.experimental.pallas import tpu as pltpu
from jax.sharding import PartitionSpec as P

F32 = jnp.float32
BF16 = jnp.bfloat16
BANDS = 4
SECTORS = 32
BIG = 24 << 20


def mesh_pairs(partner):
    return [
        (b * SECTORS + s, (lambda t: t[0] * SECTORS + t[1] % SECTORS)(partner(b, s)))
        for b in range(BANDS)
        for s in range(SECTORS)
    ]


LON_EVEN = mesh_pairs(lambda b, s: (b, s ^ 1))
LON_ODD = mesh_pairs(lambda b, s: (b, s + 1 if s % 2 else s - 1))
LAT_OUTER = mesh_pairs(
    lambda b, s: {0: (0, s + 16), 1: (2, s), 2: (1, s), 3: (3, s + 16)}[b]
)
LAT_INNER = mesh_pairs(lambda b, s: (b ^ 1, s))


def exchange(block, pairs):
    return lax.ppermute(block, ("lat", "lon"), pairs)


def nt_dot(a, b):
    return lax.dot_general(a, b, (((1,), (1,)), ((), ())), preferred_element_type=F32)


def group_ones(size, width):
    rows = lax.broadcasted_iota(jnp.int32, (size, size), 0) // width
    cols = lax.broadcasted_iota(jnp.int32, (size, size), 1) // width
    return (rows == cols).astype(F32).astype(BF16)


def norm_gelu(v, gain, ones, width):
    sq = v * v
    hi = sq.astype(BF16)
    lo = (sq - hi.astype(F32)).astype(BF16)
    total = jnp.dot(hi, ones, preferred_element_type=F32)
    total = total + jnp.dot(lo, ones, preferred_element_type=F32)
    x = v * lax.rsqrt(total * (1.0 / width) + 1e-05) * gain
    return jax.nn.gelu(x, approximate=True)


def unit(size):
    rows = lax.broadcasted_iota(jnp.int32, (size, size), 0)
    cols = lax.broadcasted_iota(jnp.int32, (size, size), 1)
    return (rows == cols).astype(F32).astype(BF16)


HBM = pl.BlockSpec(memory_space=pltpu.HBM)
SMEM = pl.BlockSpec(memory_space=pltpu.SMEM)
VMEM = pl.BlockSpec(memory_space=pltpu.VMEM)


def in_hbm(x):
    return pltpu.with_memory_space_constraint(x, pltpu.HBM)


def half_lanes():
    lanes = lax.broadcasted_iota(jnp.int32, (16, 128), 1)
    low = (lanes < 64).astype(F32).astype(BF16)
    high = (lanes >= 64).astype(F32).astype(BF16)
    return low, high


def send_sides(m0_ref, m1_ref, east, west):
    odd = lax.axis_index("lon") % 2

    def fill(east_ref, west_ref):
        for q in range(32):
            east_ref[q] = east(q).astype(BF16)
            west_ref[q] = west(q).astype(BF16)

    @pl.when(odd == 0)
    def _():
        fill(m0_ref, m1_ref)

    @pl.when(odd == 1)
    def _():
        fill(m1_ref, m0_ref)


def border_kernel(btarget, x_hbm, w_hbm, m0_ref, m1_ref, token, xv, wv, st, sb, acc, sem):
    states = pltpu.make_async_copy(x_hbm, xv, sem.at[4])
    states.start()
    chunks = [
        pltpu.make_async_copy(
            w_hbm.at[pl.ds(32 * c, 32)], wv.at[pl.ds(32 * c, 32)], sem.at[c]
        )
        for c in range(4)
    ]
    for c in chunks:
        c.start()
    acc[...] = jnp.zeros_like(acc)
    low, high = half_lanes()
    eye = unit(128)
    states.wait()
    for c in range(0, 16, 2):
        x = jnp.concatenate([xv[c], xv[c + 16], xv[c + 1], xv[c + 17]], axis=0)
        out = nt_dot(eye, x)
        st[pl.ds(c, 128, stride=16), :] = out[:, :128]
        st[pl.ds(c + 1, 128, stride=16), :] = out[:, 128:]
    for q in range(8):
        sb[16 * q : 16 * q + 16] = st[256 * q : 256 * q + 256].astype(BF16).reshape(16, 16, 128)
    for c in range(4):
        chunks[c].wait()

        def body(carry, c=c):
            n0 = 32 * c
            vals = []
            for u in range(0, 32, 2):
                rows = [sb[n0 + u + k] * half for k in range(2) for half in (low, high)]
                w = jnp.concatenate([wv[n0 + u], wv[n0 + u + 1]], axis=1)
                rhs = jnp.concatenate([w, w], axis=0)
                vals.append(
                    jnp.dot(jnp.concatenate(rows, axis=0), rhs, preferred_element_type=F32)
                )
            for u in range(32):
                k = u % 2
                acc[btarget[n0 + u]] += vals[u // 2][32 * k : 32 * k + 32, 128 * k : 128 * k + 128]
            return carry

        body(0)
    send_sides(m0_ref, m1_ref, lambda q: acc[32 + q], lambda q: acc[q])
    token[...] = jnp.zeros_like(token)


def border_sums(btarget, bstate, bweight):
    side = jax.ShapeDtypeStruct((32, 32, 128), BF16)
    return pl.pallas_call(
        border_kernel,
        name="border_sums",
        in_specs=[SMEM, HBM, HBM],
        out_specs=[VMEM, VMEM, VMEM],
        out_shape=[side, side, jax.ShapeDtypeStruct((8, 128), F32)],
        scratch_shapes=[
            pltpu.VMEM((32, 64, 128), BF16),
            pltpu.VMEM((128, 64, 128), BF16),
            pltpu.VMEM((2048, 128), F32),
            pltpu.VMEM((128, 16, 128), BF16),
            pltpu.VMEM((64, 32, 128), F32),
            pltpu.SemaphoreType.DMA((5,)),
        ],
        cost_estimate=pl.CostEstimate(
            flops=2 * 128 * 32 * 64 * 128, bytes_accessed=4 << 20, transcendentals=0
        ),
        compiler_params=pltpu.CompilerParams(vmem_limit_bytes=BIG),
    )(btarget, in_hbm(jnp.transpose(bstate, (1, 2, 0))), in_hbm(bweight))


def sums_kernel(
    target, count, after, x_hbm, w_hbm, acc_ref, m0_ref, m1_ref, xv, wv, st, sb, xsem, wsem
):
    states = [
        pltpu.make_async_copy(x_hbm.at[:, :, pl.ds(256 * p, 256)], xv.at[p], xsem.at[p])
        for p in range(2)
    ]
    chunks = {
        (p, c, h): pltpu.make_async_copy(
            w_hbm.at[pl.ds(256 * p + 128 * h + 32 * c, 32)],
            wv.at[pl.ds(256 * p + 128 * h + 32 * c, 32)],
            wsem.at[p, c, h],
        )
        for p in range(2)
        for c in range(4)
        for h in range(2)
    }
    for p in range(2):
        states[p].start()
    for c in chunks.values():
        c.start()
    low, high = half_lanes()
    low = jnp.concatenate([low, low], axis=0)
    high = jnp.concatenate([high, high], axis=0)
    eye = unit(128)
    for p in range(2):
        states[p].wait()
        for c in range(0, 32, 2):
            x = jnp.concatenate(
                [xv[p, c + k, :, 128 * h : 128 * h + 128] for k in range(2) for h in range(2)], axis=0
            )
            out = nt_dot(eye, x)
            st[pl.ds(c, 128, stride=32), :] = out[:, :128]
            st[pl.ds(c + 1, 128, stride=32), :] = out[:, 128:]
        for q in range(16):
            sb[128 * p + 8 * q : 128 * p + 8 * q + 8] = (
                st[256 * q : 256 * q + 256].astype(BF16).reshape(8, 32, 128)
            )
    for p in range(2):
        for c in range(4):
            for h in range(2):
                chunks[p, c, h].wait()
        for u in range(0, 128, 2):
            rows = [sb[128 * p + u + k] * half for k in range(2) for half in (low, high)]
            cols = [[wv[256 * p + 128 * h + u + k] for k in range(2)] for h in range(2)]
            rhs = jnp.concatenate([jnp.concatenate(r, axis=1) for r in cols], axis=0)
            both = jnp.dot(jnp.concatenate(rows, axis=0), rhs, preferred_element_type=F32)
            for k in range(2):
                for h in range(2):
                    n = 256 * p + 128 * h + u + k
                    at = 64 * k + 32 * h
                    v = both[at : at + 32, 128 * k : 128 * k + 128]
                    if p == 0:
                        acc_ref[target[n]] = v
                    else:
                        acc_ref[jnp.where(n < count[0], target[n], 256)] += v
    send_sides(m0_ref, m1_ref, lambda q: acc_ref[8 * q + 7], lambda q: acc_ref[8 * q])


def inner_sums(target, count, after, state, weight):
    side = jax.ShapeDtypeStruct((32, 32, 128), BF16)
    return pl.pallas_call(
        sums_kernel,
        name="inner_sums",
        in_specs=[SMEM, SMEM, VMEM, HBM, HBM],
        out_specs=[VMEM, VMEM, VMEM],
        out_shape=[pltpu.VMEM((257, 32, 128), F32), side, side],
        scratch_shapes=[
            pltpu.VMEM((2, 32, 64, 256), BF16),
            pltpu.VMEM((512, 64, 128), BF16),
            pltpu.VMEM((4096, 128), F32),
            pltpu.VMEM((256, 32, 128), BF16),
            pltpu.SemaphoreType.DMA((2,)),
            pltpu.SemaphoreType.DMA((2, 4, 2)),
        ],
        cost_estimate=pl.CostEstimate(
            flops=2 * 512 * 32 * 64 * 128, bytes_accessed=16 << 20, transcendentals=0
        ),
        compiler_params=pltpu.CompilerParams(vmem_limit_bytes=BIG),
    )(target, count, after, in_hbm(jnp.transpose(state, (1, 2, 0))), in_hbm(weight))


def weights_kernel(k1_ref, k2_ref, b1_ref, g1_ref, b2_ref, g2_ref, w1_ref, w2_ref, v_ref):
    w1_ref[...] = jnp.zeros_like(w1_ref)
    w2_ref[...] = jnp.zeros_like(w2_ref)
    for r in range(7):
        for s in range(7):
            for t in range(4):
                row = r * 512 + (2 * t + s + 1) * 32
                w1_ref[row : row + 32, t * 64 : (t + 1) * 64] = k1_ref[r * 7 + s]
            for t in range(2):
                row = r * 640 + (2 * t + s + 1) * 64
                w2_ref[row : row + 64, t * 128 : (t + 1) * 128] = k2_ref[r * 7 + s]
    for t in range(4):
        v_ref[0:1, t * 64 : (t + 1) * 64] = b1_ref[...]
        v_ref[1:2, t * 64 : (t + 1) * 64] = g1_ref[...]
    for t in range(2):
        v_ref[2:3, t * 128 : (t + 1) * 128] = b2_ref[...]
        v_ref[3:4, t * 128 : (t + 1) * 128] = g2_ref[...]


def matrix_weights(k1, k2, b1, g1, b2, g2):
    return pl.pallas_call(
        weights_kernel,
        name="matrix_weights",
        out_shape=[
            jax.ShapeDtypeStruct((3584, 256), BF16),
            jax.ShapeDtypeStruct((4480, 256), BF16),
            jax.ShapeDtypeStruct((8, 256), F32),
        ],
        cost_estimate=pl.CostEstimate(flops=0, bytes_accessed=8 << 20, transcendentals=0),
        compiler_params=pltpu.CompilerParams(vmem_limit_bytes=16 << 20),
    )(k1.reshape(49, 32, 64), k2.reshape(49, 64, 128), b1[None], g1[None], b2[None], g2[None])


def field_kernel(
    acc, rb0_ref, rb1_ref, ri0_ref, ri1_ref, m0_ref, m1_ref, f_ref, e_ref, ma_ref, mb_ref, fs, et
):
    odd = lax.axis_index("lon") % 2
    upper = lax.axis_index("lat") % 2
    rows = lax.broadcasted_iota(jnp.int32, (32, 128), 0)
    pix = lax.broadcasted_iota(jnp.int32, (32, 128), 1)
    pick = (pix // 4 == (rows % 8) * 4 + rows // 8).astype(F32).astype(BF16)
    keep = (
        lax.broadcasted_iota(jnp.int32, (128, 128), 0) // 32
        == lax.broadcasted_iota(jnp.int32, (128, 128), 1) % 4
    ).astype(F32).astype(BF16)
    f_ref[:, 0:2] = jnp.zeros((4, 2, 2, 16, 128), BF16)
    f_ref[:, 130:132] = jnp.zeros((4, 2, 2, 16, 128), BF16)
    et[...] = jnp.zeros_like(et)
    is_odd = odd == 1

    def step(i, carry):
        for y in range(4):
            east_border = jnp.where(is_odd, rb1_ref[4 * i + y], rb0_ref[4 * i + y]).astype(F32)
            east_inner = jnp.where(is_odd, ri1_ref[4 * i + y], ri0_ref[4 * i + y]).astype(F32)
            west_border = jnp.where(is_odd, rb0_ref[4 * i + y], rb1_ref[4 * i + y]).astype(F32)
            west_inner = jnp.where(is_odd, ri0_ref[4 * i + y], ri1_ref[4 * i + y]).astype(F32)
            own_east = jnp.where(is_odd, m1_ref[4 * i + y], m0_ref[4 * i + y]).astype(F32)
            own_west = jnp.where(is_odd, m0_ref[4 * i + y], m1_ref[4 * i + y]).astype(F32)
            patches = [acc[32 * i + 8 * y + c] for c in range(8)]
            patches[0] = patches[0] + west_border
            patches[7] = patches[7] + east_border
            patches = [west_inner + own_west] + patches + [east_inner + own_east]
            for c in range(0, 10, 2):
                pair = [patches[c].astype(BF16), patches[c + 1].astype(BF16)]
                spread = jnp.concatenate(
                    [jnp.concatenate([v] * 4, axis=0) * keep for v in pair], axis=0
                )
                both = nt_dot(pick, spread)
                for h in range(2):
                    pc = c + h - 1
                    for k in range(4):
                        v = both[8 * k : 8 * k + 8, 128 * h : 128 * h + 128]
                        g = 2 * pc + k // 2
                        kk = 4 * pc + k
                        if 0 <= pc < 8:
                            fs[y, k % 2, pl.ds(g, 8, stride=16), :] = v
                        if k % 2 == 0 and 1 <= g <= 16:
                            fs[y, 3, pl.ds(g - 1, 8, stride=16), :] = v
                        if k % 2 == 1 and -1 <= g <= 14:
                            fs[y, 2, pl.ds(g + 1, 8, stride=16), :] = v
                        if kk in (-3, -2, -1, 0, 31, 32, 33):
                            slot = kk + 3 if kk <= 0 else kk - 27
                            e_ref[slot, pl.ds(8 + 32 * i + 8 * y, 8), :] = v
                            et[y, pl.ds(slot, 8, stride=16), :] = v
            for a in range(4):
                f_ref[a, pl.ds(2 + 16 * i + 4 * y, 4)] = fs[y, a].astype(BF16).reshape(4, 2, 16, 128)

        def send(ref, first, start):
            for a in range(4):
                ref[a] = f_ref[a, 2 + start + first : 2 + start + first + 5]
            for q in range(5):
                y, o = (first + q) // 4, (first + q) % 4
                ref[4, q] = et[y, 32 * o : 32 * o + 32].astype(BF16).reshape(2, 16, 128)

        @pl.when((i == 0) & (upper == 0))
        def _():
            send(ma_ref, 0, 0)

        @pl.when((i == 0) & (upper == 1))
        def _():
            send(mb_ref, 0, 0)

        @pl.when((i == 7) & (upper == 0))
        def _():
            send(mb_ref, 11, 112)

        @pl.when((i == 7) & (upper == 1))
        def _():
            send(ma_ref, 11, 112)

        return carry

    lax.fori_loop(0, 8, step, 0)


def build_field(acc, *sides):
    msg = jax.ShapeDtypeStruct((5, 5, 2, 16, 128), BF16)
    return pl.pallas_call(
        field_kernel,
        name="build_field",
        in_specs=[VMEM] * 7,
        out_specs=[VMEM] * 4,
        out_shape=[
            pltpu.VMEM((4, 132, 2, 16, 128), BF16),
            pltpu.VMEM((7, 272, 128), F32),
            msg,
            msg,
        ],
        scratch_shapes=[
            pltpu.VMEM((4, 4, 128, 128), F32),
            pltpu.VMEM((4, 128, 128), F32),
        ],
        compiler_params=pltpu.CompilerParams(vmem_limit_bytes=24 << 20),
    )(acc, *sides)


ORDER = (2, 0, 1, 3)


TILE = 32


def first_kernel(f_ref, e_ref, w_ref, v_ref, h_ref, raw, edge, hs, ms, el):
    ones = group_ones(256, 64)
    many = TILE * 16
    tiles = 128 // TILE

    def mix(lhs):
        return jnp.dot(lhs, w_ref[...], preferred_element_type=F32) + v_ref[0:1]

    def side(n):
        parts = []
        for r in range(7):
            for j in range(4):
                slot = 4 * n + j
                if slot == 7:
                    parts.append(jnp.zeros((128, 128), BF16))
                else:
                    parts.append(e_ref[slot, pl.ds(8 - 3 + r, 128, stride=2), :].astype(BF16))
        return jnp.concatenate(parts, axis=1)

    def start(i):
        parts = []
        for r in range(7):
            for a in ORDER:
                first = TILE * i + (r + 1) // 2
                x = f_ref[a, first : first + TILE, (r + 1) % 2]
                parts.append(x.reshape(many, 128))
        raw[i] = mix(jnp.concatenate(parts, axis=1))

    def finish(i):
        h = norm_gelu(raw[i], v_ref[1:2], ones, 64)
        for c in range(2):
            hs[i, c, 8 : 8 + many] = h[:, 128 * c : 128 * c + 128]
        ms[i, 0] = hs[i, 0, 7 : 7 + many]
        ms[i, 1] = hs[i, 1, 7 : 7 + many]
        ms[i, 2] = hs[i, 0, 9 : 9 + many]
        rows = slice(TILE * i, TILE * i + TILE)
        ms[i, 0, pl.ds(0, TILE, stride=16), :] = el[0, rows, 0:128]
        ms[i, 1, pl.ds(0, TILE, stride=16), :] = el[0, rows, 128:256]
        ms[i, 2, pl.ds(15, TILE, stride=16), :] = el[1, rows, 0:128]
        half = TILE // 2
        tile = lambda v: v.astype(BF16).reshape(half, 2, 16, 128)
        to = slice(half * i, half * i + half)
        h_ref[0, to] = tile(ms[i, 0])
        h_ref[1, to] = tile(ms[i, 1])
        h_ref[2, to] = tile(hs[i, 0, 8 : 8 + many])
        h_ref[3, to] = tile(hs[i, 1, 8 : 8 + many])
        h_ref[4, to] = tile(ms[i, 2])

    edge[...] = mix(jnp.concatenate([side(0), side(1)], axis=0))
    start(0)
    out = norm_gelu(edge[...], v_ref[1:2], ones, 64)
    el[0] = out[0:128]
    el[1] = out[128:256]
    for i in range(tiles):
        if i + 1 < tiles:
            start(i + 1)
        finish(i)


def first_conv(f, e, w1, vec):
    tiles = 128 // TILE
    many = TILE * 16
    return pl.pallas_call(
        first_kernel,
        name="first_conv",
        in_specs=[VMEM] * 4,
        out_specs=VMEM,
        out_shape=pltpu.VMEM((5, 64, 2, 16, 128), BF16),
        scratch_shapes=[
            pltpu.VMEM((tiles, many, 256), F32),
            pltpu.VMEM((256, 256), F32),
            pltpu.VMEM((tiles, 2, many + 16, 128), F32),
            pltpu.VMEM((tiles, 3, many, 128), F32),
            pltpu.VMEM((2, 128, 256), F32),
        ],
        cost_estimate=pl.CostEstimate(
            flops=2 * 2304 * 3584 * 256, bytes_accessed=12 << 20, transcendentals=1 << 20
        ),
        compiler_params=pltpu.CompilerParams(vmem_limit_bytes=28 << 20),
    )(f, e, w1, vec)


BASES = (0, 2, 4, 11, 13, 20, 27, 29)


def second_kernel(
    h_ref, ma_ref, mb_ref, ra_ref, rb_ref, w1_ref, w2_ref, v_ref,
    o_ref, top, bot, ve, vf, le, ts, ms, raw, os,
):
    lat = lax.axis_index("lat")
    odd = lat % 2 == 1
    north = lat == 0
    south = lat == 3
    ones1 = group_ones(256, 64)
    ones2 = group_ones(256, 128)

    def window(ref, first, count):
        parts = []
        for r in range(7):
            for a in range(5):
                at = first + (r + 1) // 2
                parts.append(ref[a, at : at + count, (r + 1) % 2].reshape(16 * count, 128))
        return jnp.concatenate(parts, axis=1)

    def mix(lhs):
        return jnp.dot(lhs, w2_ref[...], preferred_element_type=F32) + v_ref[2:3]

    def finish(n, at, first, count):
        y = norm_gelu(raw[n, at : at + 16 * count], v_ref[3:4], ones2, 128)
        for t in range(2):
            os[n, pl.ds(2 * at + t, 16 * count, stride=2), :] = y[:, 128 * t : 128 * t + 128]
        o_ref[first : first + count] = (
            os[n, 2 * at : 2 * at + 32 * count].astype(BF16).reshape(count, 32, 128)
        )

    def row(ref, a, m):
        return ref[a, m // 2, m % 2]

    def own_top(a, m):
        return jnp.where(odd, row(mb_ref, a, m), row(ma_ref, a, m))

    def own_bot(a, m):
        return jnp.where(odd, row(ma_ref, a, m), row(mb_ref, a, m))

    def halo_top(a, m):
        return jnp.where(odd, row(rb_ref, a, m), row(ra_ref, a, m))

    def halo_bot(a, m):
        return jnp.where(odd, row(ra_ref, a, m), row(rb_ref, a, m))

    for a in range(5):
        def put(n, v):
            if a < 4:
                vf[a, n] = v
            else:
                ve[16 * n : 16 * n + 16] = v.astype(F32)

        for q in range(11):
            normal = halo_top(a, q + 1) if q < 9 else own_top(a, q - 9)
            polar = own_top(a, 2 - q) if q < 3 else halo_top(a, q - 3)
            put(q, jnp.where(north, polar, normal))
        for q in range(9):
            if q < 3:
                v = jnp.where(north, halo_top(a, 2 - q), halo_top(a, 7 + q))
            else:
                v = own_top(a, q - 3)
            put(11 + q, v)
        for q in range(7):
            if q < 5:
                v = own_bot(a, 5 + q)
            else:
                v = jnp.where(south, halo_bot(a, 14 - q), halo_bot(a, q - 5))
            put(20 + q, v)
        for q in range(9):
            normal = own_bot(a, 7 + q) if q < 3 else halo_bot(a, q - 3)
            polar = halo_bot(a, 3 + q) if q < 7 else own_bot(a, 16 - q)
            put(27 + q, jnp.where(south, polar, normal))

    for n, base in enumerate(BASES):
        for r in range(7):
            for j in range(4):
                col = 128 * (4 * r + j)
                for side in range(2):
                    src = 16 * (base + r) + 4 * side + j
                    le[n + 8 * side : n + 8 * side + 1, col : col + 128] = ve[src : src + 1, :]
    parts = []
    for r in range(7):
        for a in ORDER:
            parts.append(jnp.concatenate([vf[a, base + r] for base in BASES], axis=0))
    lhs = jnp.concatenate([jnp.concatenate(parts, axis=1), le[...].astype(BF16)], axis=0)
    ts[2] = jnp.dot(lhs, w1_ref[...], preferred_element_type=F32) + v_ref[0:1]
    raw[0] = mix(window(h_ref, 14, 32))
    for a in range(5):
        top[a, 2:20] = h_ref[a, 0:18]
        bot[a, 0:18] = h_ref[a, 46:64]
    h = norm_gelu(ts[2], v_ref[1:2], ones1, 64)
    for c in range(2):
        ts[c, 8:136, 0:128] = h[0:128, 128 * c : 128 * c + 128]
    ms[0] = ts[0, 7:135, 0:128]
    ms[1] = ts[1, 7:135, 0:128]
    ms[2] = ts[0, 9:137, 0:128]
    ms[0, pl.ds(0, 8, stride=16), :] = h[128:136, 0:128]
    ms[1, pl.ds(0, 8, stride=16), :] = h[128:136, 128:256]
    ms[2, pl.ds(15, 8, stride=16), :] = h[136:144, 0:128]
    full = [ms[0], ms[1], ts[0, 8:136, 0:128], ts[1, 8:136, 0:128], ms[2]]
    for a in range(5):
        v = full[a].astype(BF16).reshape(8, 16, 128)
        top[a, 0, 1] = jnp.where(north, v[2], v[0])
        top[a, 1, 0] = v[1]
        top[a, 1, 1] = jnp.where(north, v[0], v[2])
        top[a, 2, 0] = v[3]
        top[a, 2, 1] = v[4]
        bot[a, 17, 1] = v[5]
        bot[a, 18, 0] = jnp.where(south, v[7], v[6])
        bot[a, 18, 1] = jnp.where(south, v[6], v[7])
    raw[1] = mix(jnp.concatenate([window(top, 0, 16), window(bot, 0, 16)], axis=0))
    finish(0, 0, 16, 32)
    finish(1, 0, 0, 16)
    finish(1, 256, 48, 16)


def second_conv(h, ma, mb, ra, rb, w1, w2, vec):
    return pl.pallas_call(
        second_kernel,
        name="second_conv",
        in_specs=[VMEM] * 8,
        out_specs=VMEM,
        out_shape=jax.ShapeDtypeStruct((64, 32, 128), BF16),
        scratch_shapes=[
            pltpu.VMEM((5, 20, 2, 16, 128), BF16),
            pltpu.VMEM((5, 20, 2, 16, 128), BF16),
            pltpu.VMEM((36 * 16, 128), F32),
            pltpu.VMEM((4, 36, 16, 128), BF16),
            pltpu.VMEM((16, 3584), F32),
            pltpu.VMEM((3, 144, 256), F32),
            pltpu.VMEM((3, 128, 128), F32),
            pltpu.VMEM((2, 512, 256), F32),
            pltpu.VMEM((2, 1024, 128), F32),
        ],
        compiler_params=pltpu.CompilerParams(vmem_limit_bytes=28 << 20),
    )(h, ma, mb, ra, rb, w1, w2, vec)


def local(
    cell_state,
    remap_weight,
    block_target,
    block_count,
    border_state,
    border_weight,
    border_target,
    kernel_one,
    bias_one,
    gain_one,
    kernel_two,
    bias_two,
    gain_two,
):
    m0, m1, after = border_sums(border_target[0, 0], border_state[0, 0], border_weight[0, 0])
    rb0 = exchange(m0, LON_EVEN)
    rb1 = exchange(m1, LON_ODD)
    acc, i0, i1 = inner_sums(
        block_target[0, 0], block_count[0], after, cell_state[0, 0], remap_weight[0, 0]
    )
    ri0 = exchange(i0, LON_EVEN)
    ri1 = exchange(i1, LON_ODD)
    w1, w2, vec = matrix_weights(kernel_one, kernel_two, bias_one, gain_one, bias_two, gain_two)
    f, e, ma, mb = build_field(acc, rb0, rb1, ri0, ri1, m0, m1)
    ra = exchange(ma, LAT_OUTER)
    rb = exchange(mb, LAT_INNER)
    h = first_conv(f, e, w1, vec)
    return second_conv(h, ma, mb, ra, rb, w1, w2, vec)


def solution(mesh):
    placed = (
        P("lat", "lon", None, None, None),
        P("lat", "lon", None, None, None),
        P("lat", "lon", None),
        P("lat", "lon"),
        P("lat", "lon", None, None, None),
        P("lat", "lon", None, None, None),
        P("lat", "lon", None),
        P(),
        P(),
        P(),
        P(),
        P(),
        P(),
    )
    return jax.shard_map(
        local, mesh=mesh, in_specs=placed, out_specs=P("lat", "lon", None), check_vma=False
    )
```

```python
import jax
import jax.numpy as jnp
from jax import lax
from jax.experimental import pallas as pl
from jax.experimental.pallas import tpu as pltpu
from jax.sharding import PartitionSpec as P

F32 = jnp.float32
BF16 = jnp.bfloat16
BANDS = 4
SECTORS = 32
BIG = 24 << 20


def mesh_pairs(partner):
    return [
        (b * SECTORS + s, (lambda t: t[0] * SECTORS + t[1] % SECTORS)(partner(b, s)))
        for b in range(BANDS)
        for s in range(SECTORS)
    ]


LON_EVEN = mesh_pairs(lambda b, s: (b, s ^ 1))
LON_ODD = mesh_pairs(lambda b, s: (b, s + 1 if s % 2 else s - 1))
LAT_OUTER = mesh_pairs(
    lambda b, s: {0: (0, s + 16), 1: (2, s), 2: (1, s), 3: (3, s + 16)}[b]
)
LAT_INNER = mesh_pairs(lambda b, s: (b ^ 1, s))


def exchange(block, pairs):
    return lax.ppermute(block, ("lat", "lon"), pairs)


def nt_dot(a, b):
    return lax.dot_general(a, b, (((1,), (1,)), ((), ())), preferred_element_type=F32)


def group_ones(size, width):
    rows = lax.broadcasted_iota(jnp.int32, (size, size), 0) // width
    cols = lax.broadcasted_iota(jnp.int32, (size, size), 1) // width
    return (rows == cols).astype(F32).astype(BF16)


def norm_gelu(v, gain, ones, width):
    sq = v * v
    hi = sq.astype(BF16)
    lo = (sq - hi.astype(F32)).astype(BF16)
    total = jnp.dot(hi, ones, preferred_element_type=F32)
    total = total + jnp.dot(lo, ones, preferred_element_type=F32)
    x = v * lax.rsqrt(total * (1.0 / width) + 1e-05) * gain
    return jax.nn.gelu(x, approximate=True)


def unit(size):
    rows = lax.broadcasted_iota(jnp.int32, (size, size), 0)
    cols = lax.broadcasted_iota(jnp.int32, (size, size), 1)
    return (rows == cols).astype(F32).astype(BF16)


HBM = pl.BlockSpec(memory_space=pltpu.HBM)
SMEM = pl.BlockSpec(memory_space=pltpu.SMEM)
VMEM = pl.BlockSpec(memory_space=pltpu.VMEM)


def in_hbm(x):
    return pltpu.with_memory_space_constraint(x, pltpu.HBM)


def half_lanes():
    lanes = lax.broadcasted_iota(jnp.int32, (16, 128), 1)
    low = (lanes < 64).astype(F32).astype(BF16)
    high = (lanes >= 64).astype(F32).astype(BF16)
    return low, high


def send_sides(m0_ref, m1_ref, east, west):
    odd = lax.axis_index("lon") % 2

    def fill(east_ref, west_ref):
        for q in range(32):
            east_ref[q] = east(q).astype(BF16)
            west_ref[q] = west(q).astype(BF16)

    @pl.when(odd == 0)
    def _():
        fill(m0_ref, m1_ref)

    @pl.when(odd == 1)
    def _():
        fill(m1_ref, m0_ref)


def border_kernel(
    btarget_hbm, x_hbm, w_hbm, m0_ref, m1_ref, token, xv, wv, st, sb, acc, btarget, sem
):
    states = pltpu.make_async_copy(x_hbm, xv, sem.at[4])
    states.start()
    targets = pltpu.make_async_copy(btarget_hbm, btarget, sem.at[5])
    targets.start()
    chunks = [
        pltpu.make_async_copy(
            w_hbm.at[pl.ds(32 * c, 32)], wv.at[pl.ds(32 * c, 32)], sem.at[c]
        )
        for c in range(4)
    ]
    for c in chunks:
        c.start()
    acc[...] = jnp.zeros_like(acc)
    low, high = half_lanes()
    eye = unit(128)
    states.wait()
    for c in range(0, 16, 2):
        x = jnp.concatenate([xv[c], xv[c + 16], xv[c + 1], xv[c + 17]], axis=0)
        out = nt_dot(eye, x)
        st[pl.ds(c, 128, stride=16), :] = out[:, :128]
        st[pl.ds(c + 1, 128, stride=16), :] = out[:, 128:]
    for q in range(8):
        sb[16 * q : 16 * q + 16] = st[256 * q : 256 * q + 256].astype(BF16).reshape(16, 16, 128)
    targets.wait()
    for c in range(4):
        chunks[c].wait()

        def body(carry, c=c):
            n0 = 32 * c
            vals = []
            for u in range(0, 32, 2):
                rows = [sb[n0 + u + k] * half for k in range(2) for half in (low, high)]
                w = jnp.concatenate([wv[n0 + u], wv[n0 + u + 1]], axis=1)
                rhs = jnp.concatenate([w, w], axis=0)
                vals.append(
                    jnp.dot(jnp.concatenate(rows, axis=0), rhs, preferred_element_type=F32)
                )
            for u in range(32):
                k = u % 2
                acc[btarget[n0 + u]] += vals[u // 2][32 * k : 32 * k + 32, 128 * k : 128 * k + 128]
            return carry

        body(0)
    send_sides(m0_ref, m1_ref, lambda q: acc[32 + q], lambda q: acc[q])
    token[...] = jnp.zeros_like(token)


def border_sums(btarget, bstate, bweight):
    side = jax.ShapeDtypeStruct((32, 32, 128), BF16)
    return pl.pallas_call(
        border_kernel,
        name="border_sums",
        in_specs=[HBM, HBM, HBM],
        out_specs=[VMEM, VMEM, VMEM],
        out_shape=[side, side, jax.ShapeDtypeStruct((8, 128), F32)],
        scratch_shapes=[
            pltpu.VMEM((32, 64, 128), BF16),
            pltpu.VMEM((128, 64, 128), BF16),
            pltpu.VMEM((2048, 128), F32),
            pltpu.VMEM((128, 16, 128), BF16),
            pltpu.VMEM((64, 32, 128), F32),
            pltpu.SMEM((128,), jnp.int32),
            pltpu.SemaphoreType.DMA((6,)),
        ],
        cost_estimate=pl.CostEstimate(
            flops=2 * 128 * 32 * 64 * 128, bytes_accessed=4 << 20, transcendentals=0
        ),
        compiler_params=pltpu.CompilerParams(vmem_limit_bytes=BIG),
    )(in_hbm(btarget), in_hbm(jnp.transpose(bstate, (1, 2, 0))), in_hbm(bweight))


def sums_kernel(
    target, count, after, x_hbm, w_hbm, acc_ref, m0_ref, m1_ref, xv, wv, st, sb, xsem, wsem
):
    states = [
        pltpu.make_async_copy(x_hbm.at[:, :, pl.ds(256 * p, 256)], xv.at[p], xsem.at[p])
        for p in range(2)
    ]
    chunks = {
        (p, c, h): pltpu.make_async_copy(
            w_hbm.at[pl.ds(256 * p + 128 * h + 32 * c, 32)],
            wv.at[pl.ds(256 * p + 128 * h + 32 * c, 32)],
            wsem.at[p, c, h],
        )
        for p in range(2)
        for c in range(4)
        for h in range(2)
    }
    for p in range(2):
        states[p].start()
    for c in chunks.values():
        c.start()
    low, high = half_lanes()
    low = jnp.concatenate([low, low], axis=0)
    high = jnp.concatenate([high, high], axis=0)
    eye = unit(128)
    for p in range(2):
        states[p].wait()
        for c in range(0, 32, 2):
            x = jnp.concatenate(
                [xv[p, c + k, :, 128 * h : 128 * h + 128] for k in range(2) for h in range(2)], axis=0
            )
            out = nt_dot(eye, x)
            st[pl.ds(c, 128, stride=32), :] = out[:, :128]
            st[pl.ds(c + 1, 128, stride=32), :] = out[:, 128:]
        for q in range(16):
            sb[128 * p + 8 * q : 128 * p + 8 * q + 8] = (
                st[256 * q : 256 * q + 256].astype(BF16).reshape(8, 32, 128)
            )
    for p in range(2):
        for c in range(4):
            for h in range(2):
                chunks[p, c, h].wait()
        for u in range(0, 128, 2):
            rows = [sb[128 * p + u + k] * half for k in range(2) for half in (low, high)]
            cols = [[wv[256 * p + 128 * h + u + k] for k in range(2)] for h in range(2)]
            rhs = jnp.concatenate([jnp.concatenate(r, axis=1) for r in cols], axis=0)
            both = jnp.dot(jnp.concatenate(rows, axis=0), rhs, preferred_element_type=F32)
            for k in range(2):
                for h in range(2):
                    n = 256 * p + 128 * h + u + k
                    at = 64 * k + 32 * h
                    v = both[at : at + 32, 128 * k : 128 * k + 128]
                    if p == 0:
                        acc_ref[target[n]] = v
                    else:
                        acc_ref[jnp.where(n < count[0], target[n], 256)] += v
    send_sides(m0_ref, m1_ref, lambda q: acc_ref[8 * q + 7], lambda q: acc_ref[8 * q])


def inner_sums(target, count, after, state, weight):
    side = jax.ShapeDtypeStruct((32, 32, 128), BF16)
    return pl.pallas_call(
        sums_kernel,
        name="inner_sums",
        in_specs=[SMEM, SMEM, VMEM, HBM, HBM],
        out_specs=[VMEM, VMEM, VMEM],
        out_shape=[pltpu.VMEM((257, 32, 128), F32), side, side],
        scratch_shapes=[
            pltpu.VMEM((2, 32, 64, 256), BF16),
            pltpu.VMEM((512, 64, 128), BF16),
            pltpu.VMEM((4096, 128), F32),
            pltpu.VMEM((256, 32, 128), BF16),
            pltpu.SemaphoreType.DMA((2,)),
            pltpu.SemaphoreType.DMA((2, 4, 2)),
        ],
        cost_estimate=pl.CostEstimate(
            flops=2 * 512 * 32 * 64 * 128, bytes_accessed=16 << 20, transcendentals=0
        ),
        compiler_params=pltpu.CompilerParams(vmem_limit_bytes=BIG),
    )(target, count, after, in_hbm(jnp.transpose(state, (1, 2, 0))), in_hbm(weight))


def weights_kernel(k1_ref, k2_ref, b1_ref, g1_ref, b2_ref, g2_ref, w1_ref, w2_ref, v_ref):
    w1_ref[...] = jnp.zeros_like(w1_ref)
    w2_ref[...] = jnp.zeros_like(w2_ref)
    for r in range(7):
        for s in range(7):
            for t in range(4):
                row = r * 512 + (2 * t + s + 1) * 32
                w1_ref[row : row + 32, t * 64 : (t + 1) * 64] = k1_ref[r * 7 + s]
            for t in range(2):
                row = r * 640 + (2 * t + s + 1) * 64
                w2_ref[row : row + 64, t * 128 : (t + 1) * 128] = k2_ref[r * 7 + s]
    for t in range(4):
        v_ref[0:1, t * 64 : (t + 1) * 64] = b1_ref[...]
        v_ref[1:2, t * 64 : (t + 1) * 64] = g1_ref[...]
    for t in range(2):
        v_ref[2:3, t * 128 : (t + 1) * 128] = b2_ref[...]
        v_ref[3:4, t * 128 : (t + 1) * 128] = g2_ref[...]


def matrix_weights(k1, k2, b1, g1, b2, g2):
    return pl.pallas_call(
        weights_kernel,
        name="matrix_weights",
        out_shape=[
            jax.ShapeDtypeStruct((3584, 256), BF16),
            jax.ShapeDtypeStruct((4480, 256), BF16),
            jax.ShapeDtypeStruct((8, 256), F32),
        ],
        cost_estimate=pl.CostEstimate(flops=0, bytes_accessed=8 << 20, transcendentals=0),
        compiler_params=pltpu.CompilerParams(vmem_limit_bytes=16 << 20),
    )(k1.reshape(49, 32, 64), k2.reshape(49, 64, 128), b1[None], g1[None], b2[None], g2[None])


def selectors():
    rows = lax.broadcasted_iota(jnp.int32, (32, 128), 0)
    pix = lax.broadcasted_iota(jnp.int32, (32, 128), 1)
    pick = (pix // 4 == (rows % 8) * 4 + rows // 8).astype(F32).astype(BF16)
    keep = (
        lax.broadcasted_iota(jnp.int32, (128, 128), 0) // 32
        == lax.broadcasted_iota(jnp.int32, (128, 128), 1) % 4
    ).astype(F32).astype(BF16)
    return pick, keep


def place_pair(pair, pc0, y, fs, pick, keep, edge):
    spread = jnp.concatenate(
        [jnp.concatenate([v.astype(BF16)] * 4, axis=0) * keep for v in pair], axis=0
    )
    both = nt_dot(pick, spread)
    for h in range(2):
        pc = pc0 + h
        for k in range(4):
            v = both[8 * k : 8 * k + 8, 128 * h : 128 * h + 128]
            g = 2 * pc + k // 2
            kk = 4 * pc + k
            if 0 <= pc < 8:
                fs[y, k % 2, pl.ds(g, 8, stride=16), :] = v
            if k % 2 == 0 and 1 <= g <= 16:
                fs[y, 3, pl.ds(g - 1, 8, stride=16), :] = v
            if k % 2 == 1 and -1 <= g <= 14:
                fs[y, 2, pl.ds(g + 1, 8, stride=16), :] = v
            if kk in (-3, -2, -1, 0, 31, 32, 33):
                edge(kk + 3 if kk <= 0 else kk - 27, v)


def interior_kernel(acc, f_ref, fs):
    pick, keep = selectors()
    f_ref[:, 0:2] = jnp.zeros((4, 2, 2, 16, 128), BF16)
    f_ref[:, 130:132] = jnp.zeros((4, 2, 2, 16, 128), BF16)
    fs[...] = jnp.zeros_like(fs)

    def step(i, carry):
        for y in range(4):
            for c in range(1, 7, 2):
                pair = [acc[32 * i + 8 * y + c], acc[32 * i + 8 * y + c + 1]]
                place_pair(pair, c, y, fs, pick, keep, None)
            for a in range(4):
                f_ref[a, pl.ds(2 + 16 * i + 4 * y, 4)] = fs[y, a].astype(BF16).reshape(4, 2, 16, 128)
        return carry

    lax.fori_loop(0, 8, step, 0)


def build_interior(acc):
    return pl.pallas_call(
        interior_kernel,
        name="build_interior",
        in_specs=[VMEM],
        out_specs=VMEM,
        out_shape=pltpu.VMEM((4, 132, 2, 16, 128), BF16),
        scratch_shapes=[pltpu.VMEM((4, 4, 128, 128), F32)],
        cost_estimate=pl.CostEstimate(flops=1 << 28, bytes_accessed=8 << 20, transcendentals=0),
        compiler_params=pltpu.CompilerParams(vmem_limit_bytes=16 << 20),
    )(acc)


def field_kernel(
    inside, acc, rb0_ref, rb1_ref, ri0_ref, ri1_ref, m0_ref, m1_ref,
    f_ref, e_ref, ma_ref, mb_ref, fs, et,
):
    odd = lax.axis_index("lon") % 2
    upper = lax.axis_index("lat") % 2
    pick, keep = selectors()
    et[...] = jnp.zeros_like(et)
    fs[...] = jnp.zeros_like(fs)
    is_odd = odd == 1

    def step(i, carry):
        for y in range(4):
            n = 4 * i + y
            east_border = jnp.where(is_odd, rb1_ref[n], rb0_ref[n]).astype(F32)
            east_inner = jnp.where(is_odd, ri1_ref[n], ri0_ref[n]).astype(F32)
            west_border = jnp.where(is_odd, rb0_ref[n], rb1_ref[n]).astype(F32)
            west_inner = jnp.where(is_odd, ri0_ref[n], ri1_ref[n]).astype(F32)
            own_east = jnp.where(is_odd, m1_ref[n], m0_ref[n]).astype(F32)
            own_west = jnp.where(is_odd, m0_ref[n], m1_ref[n]).astype(F32)

            def edge(slot, v, y=y):
                e_ref[slot, pl.ds(8 + 32 * i + 8 * y, 8), :] = v
                et[y, pl.ds(slot, 8, stride=16), :] = v

            west = [west_inner + own_west, acc[8 * n] + west_border]
            east = [acc[8 * n + 7] + east_border, east_inner + own_east]
            place_pair(west, -1, y, fs, pick, keep, edge)
            place_pair(east, 7, y, fs, pick, keep, edge)
            for a in range(4):
                to = pl.ds(2 + 16 * i + 4 * y, 4)
                f_ref[a, to] = inside[a, to] + fs[y, a].astype(BF16).reshape(4, 2, 16, 128)

        def send(ref, first, start):
            for a in range(4):
                ref[a] = f_ref[a, 2 + start + first : 2 + start + first + 5]
            for q in range(5):
                y, o = (first + q) // 4, (first + q) % 4
                ref[4, q] = et[y, 32 * o : 32 * o + 32].astype(BF16).reshape(2, 16, 128)

        @pl.when((i == 0) & (upper == 0))
        def _():
            send(ma_ref, 0, 0)

        @pl.when((i == 0) & (upper == 1))
        def _():
            send(mb_ref, 0, 0)

        @pl.when((i == 7) & (upper == 0))
        def _():
            send(mb_ref, 11, 112)

        @pl.when((i == 7) & (upper == 1))
        def _():
            send(ma_ref, 11, 112)

        return carry

    lax.fori_loop(0, 8, step, 0)


def build_field(inside, acc, *sides):
    msg = jax.ShapeDtypeStruct((5, 5, 2, 16, 128), BF16)
    return pl.pallas_call(
        field_kernel,
        name="build_field",
        in_specs=[VMEM] * 8,
        out_specs=[VMEM] * 4,
        out_shape=[
            pltpu.VMEM((4, 132, 2, 16, 128), BF16),
            pltpu.VMEM((7, 272, 128), F32),
            msg,
            msg,
        ],
        input_output_aliases={0: 0},
        scratch_shapes=[
            pltpu.VMEM((4, 4, 128, 128), F32),
            pltpu.VMEM((4, 128, 128), F32),
        ],
        compiler_params=pltpu.CompilerParams(vmem_limit_bytes=16 << 20),
    )(inside, acc, *sides)


ORDER = (2, 0, 1, 3)


TILE = 32


def first_kernel(f_ref, e_ref, w_ref, v_ref, h_ref, raw, edge, hs, ms, el):
    ones = group_ones(256, 64)
    many = TILE * 16
    tiles = 128 // TILE

    def mix(lhs):
        return jnp.dot(lhs, w_ref[...], preferred_element_type=F32) + v_ref[0:1]

    def side(n):
        parts = []
        for r in range(7):
            for j in range(4):
                slot = 4 * n + j
                if slot == 7:
                    parts.append(jnp.zeros((128, 128), BF16))
                else:
                    parts.append(e_ref[slot, pl.ds(8 - 3 + r, 128, stride=2), :].astype(BF16))
        return jnp.concatenate(parts, axis=1)

    def start(i):
        parts = []
        for r in range(7):
            for a in ORDER:
                first = TILE * i + (r + 1) // 2
                x = f_ref[a, first : first + TILE, (r + 1) % 2]
                parts.append(x.reshape(many, 128))
        raw[i] = mix(jnp.concatenate(parts, axis=1))

    def finish(i):
        h = norm_gelu(raw[i], v_ref[1:2], ones, 64)
        for c in range(2):
            hs[i, c, 8 : 8 + many] = h[:, 128 * c : 128 * c + 128]
        ms[i, 0] = hs[i, 0, 7 : 7 + many]
        ms[i, 1] = hs[i, 1, 7 : 7 + many]
        ms[i, 2] = hs[i, 0, 9 : 9 + many]
        rows = slice(TILE * i, TILE * i + TILE)
        ms[i, 0, pl.ds(0, TILE, stride=16), :] = el[0, rows, 0:128]
        ms[i, 1, pl.ds(0, TILE, stride=16), :] = el[0, rows, 128:256]
        ms[i, 2, pl.ds(15, TILE, stride=16), :] = el[1, rows, 0:128]
        half = TILE // 2
        tile = lambda v: v.astype(BF16).reshape(half, 2, 16, 128)
        to = slice(half * i, half * i + half)
        h_ref[0, to] = tile(ms[i, 0])
        h_ref[1, to] = tile(ms[i, 1])
        h_ref[2, to] = tile(hs[i, 0, 8 : 8 + many])
        h_ref[3, to] = tile(hs[i, 1, 8 : 8 + many])
        h_ref[4, to] = tile(ms[i, 2])

    edge[...] = mix(jnp.concatenate([side(0), side(1)], axis=0))
    start(0)
    out = norm_gelu(edge[...], v_ref[1:2], ones, 64)
    el[0] = out[0:128]
    el[1] = out[128:256]
    for i in range(tiles):
        if i + 1 < tiles:
            start(i + 1)
        finish(i)


def first_conv(f, e, w1, vec):
    tiles = 128 // TILE
    many = TILE * 16
    return pl.pallas_call(
        first_kernel,
        name="first_conv",
        in_specs=[VMEM] * 4,
        out_specs=VMEM,
        out_shape=pltpu.VMEM((5, 64, 2, 16, 128), BF16),
        scratch_shapes=[
            pltpu.VMEM((tiles, many, 256), F32),
            pltpu.VMEM((256, 256), F32),
            pltpu.VMEM((tiles, 2, many + 16, 128), F32),
            pltpu.VMEM((tiles, 3, many, 128), F32),
            pltpu.VMEM((2, 128, 256), F32),
        ],
        cost_estimate=pl.CostEstimate(
            flops=2 * 2304 * 3584 * 256, bytes_accessed=12 << 20, transcendentals=1 << 20
        ),
        compiler_params=pltpu.CompilerParams(vmem_limit_bytes=28 << 20),
    )(f, e, w1, vec)


BASES = (0, 2, 4, 11, 13, 20, 27, 29)


def second_kernel(
    h_ref, ma_ref, mb_ref, ra_ref, rb_ref, w1_ref, w2_ref, v_ref,
    o_ref, top, bot, ve, vf, le, ts, ms, raw, os,
):
    lat = lax.axis_index("lat")
    odd = lat % 2 == 1
    north = lat == 0
    south = lat == 3
    ones1 = group_ones(256, 64)
    ones2 = group_ones(256, 128)

    def window(ref, first, count):
        parts = []
        for r in range(7):
            for a in range(5):
                at = first + (r + 1) // 2
                parts.append(ref[a, at : at + count, (r + 1) % 2].reshape(16 * count, 128))
        return jnp.concatenate(parts, axis=1)

    def mix(lhs):
        return jnp.dot(lhs, w2_ref[...], preferred_element_type=F32) + v_ref[2:3]

    def finish(n, at, first, count):
        y = norm_gelu(raw[n, at : at + 16 * count], v_ref[3:4], ones2, 128)
        for t in range(2):
            os[n, pl.ds(2 * at + t, 16 * count, stride=2), :] = y[:, 128 * t : 128 * t + 128]
        o_ref[first : first + count] = (
            os[n, 2 * at : 2 * at + 32 * count].astype(BF16).reshape(count, 32, 128)
        )

    def row(ref, a, m):
        return ref[a, m // 2, m % 2]

    def own_top(a, m):
        return jnp.where(odd, row(mb_ref, a, m), row(ma_ref, a, m))

    def own_bot(a, m):
        return jnp.where(odd, row(ma_ref, a, m), row(mb_ref, a, m))

    def halo_top(a, m):
        return jnp.where(odd, row(rb_ref, a, m), row(ra_ref, a, m))

    def halo_bot(a, m):
        return jnp.where(odd, row(ra_ref, a, m), row(rb_ref, a, m))

    for a in range(5):
        def put(n, v):
            if a < 4:
                vf[a, n] = v
            else:
                ve[16 * n : 16 * n + 16] = v.astype(F32)

        for q in range(11):
            normal = halo_top(a, q + 1) if q < 9 else own_top(a, q - 9)
            polar = own_top(a, 2 - q) if q < 3 else halo_top(a, q - 3)
            put(q, jnp.where(north, polar, normal))
        for q in range(9):
            if q < 3:
                v = jnp.where(north, halo_top(a, 2 - q), halo_top(a, 7 + q))
            else:
                v = own_top(a, q - 3)
            put(11 + q, v)
        for q in range(7):
            if q < 5:
                v = own_bot(a, 5 + q)
            else:
                v = jnp.where(south, halo_bot(a, 14 - q), halo_bot(a, q - 5))
            put(20 + q, v)
        for q in range(9):
            normal = own_bot(a, 7 + q) if q < 3 else halo_bot(a, q - 3)
            polar = halo_bot(a, 3 + q) if q < 7 else own_bot(a, 16 - q)
            put(27 + q, jnp.where(south, polar, normal))

    for n, base in enumerate(BASES):
        for r in range(7):
            for j in range(4):
                col = 128 * (4 * r + j)
                for side in range(2):
                    src = 16 * (base + r) + 4 * side + j
                    le[n + 8 * side : n + 8 * side + 1, col : col + 128] = ve[src : src + 1, :]
    parts = []
    for r in range(7):
        for a in ORDER:
            parts.append(jnp.concatenate([vf[a, base + r] for base in BASES], axis=0))
    lhs = jnp.concatenate([jnp.concatenate(parts, axis=1), le[...].astype(BF16)], axis=0)
    ts[2] = jnp.dot(lhs, w1_ref[...], preferred_element_type=F32) + v_ref[0:1]
    raw[0] = mix(window(h_ref, 14, 32))
    for a in range(5):
        top[a, 2:20] = h_ref[a, 0:18]
        bot[a, 0:18] = h_ref[a, 46:64]
    h = norm_gelu(ts[2], v_ref[1:2], ones1, 64)
    for c in range(2):
        ts[c, 8:136, 0:128] = h[0:128, 128 * c : 128 * c + 128]
    ms[0] = ts[0, 7:135, 0:128]
    ms[1] = ts[1, 7:135, 0:128]
    ms[2] = ts[0, 9:137, 0:128]
    ms[0, pl.ds(0, 8, stride=16), :] = h[128:136, 0:128]
    ms[1, pl.ds(0, 8, stride=16), :] = h[128:136, 128:256]
    ms[2, pl.ds(15, 8, stride=16), :] = h[136:144, 0:128]
    full = [ms[0], ms[1], ts[0, 8:136, 0:128], ts[1, 8:136, 0:128], ms[2]]
    for a in range(5):
        v = full[a].astype(BF16).reshape(8, 16, 128)
        top[a, 0, 1] = jnp.where(north, v[2], v[0])
        top[a, 1, 0] = v[1]
        top[a, 1, 1] = jnp.where(north, v[0], v[2])
        top[a, 2, 0] = v[3]
        top[a, 2, 1] = v[4]
        bot[a, 17, 1] = v[5]
        bot[a, 18, 0] = jnp.where(south, v[7], v[6])
        bot[a, 18, 1] = jnp.where(south, v[6], v[7])
    raw[1] = mix(jnp.concatenate([window(top, 0, 16), window(bot, 0, 16)], axis=0))
    finish(0, 0, 16, 32)
    finish(1, 0, 0, 16)
    finish(1, 256, 48, 16)


def second_conv(h, ma, mb, ra, rb, w1, w2, vec):
    return pl.pallas_call(
        second_kernel,
        name="second_conv",
        in_specs=[VMEM] * 8,
        out_specs=VMEM,
        out_shape=jax.ShapeDtypeStruct((64, 32, 128), BF16),
        scratch_shapes=[
            pltpu.VMEM((5, 20, 2, 16, 128), BF16),
            pltpu.VMEM((5, 20, 2, 16, 128), BF16),
            pltpu.VMEM((36 * 16, 128), F32),
            pltpu.VMEM((4, 36, 16, 128), BF16),
            pltpu.VMEM((16, 3584), F32),
            pltpu.VMEM((3, 144, 256), F32),
            pltpu.VMEM((3, 128, 128), F32),
            pltpu.VMEM((2, 512, 256), F32),
            pltpu.VMEM((2, 1024, 128), F32),
        ],
        compiler_params=pltpu.CompilerParams(vmem_limit_bytes=28 << 20),
    )(h, ma, mb, ra, rb, w1, w2, vec)


def local(
    cell_state,
    remap_weight,
    block_target,
    block_count,
    border_state,
    border_weight,
    border_target,
    kernel_one,
    bias_one,
    gain_one,
    kernel_two,
    bias_two,
    gain_two,
):
    m0, m1, after = border_sums(border_target[0, 0], border_state[0, 0], border_weight[0, 0])
    rb0 = exchange(m0, LON_EVEN)
    rb1 = exchange(m1, LON_ODD)
    acc, i0, i1 = inner_sums(
        block_target[0, 0], block_count[0], after, cell_state[0, 0], remap_weight[0, 0]
    )
    ri0 = exchange(i0, LON_EVEN)
    ri1 = exchange(i1, LON_ODD)
    w1, w2, vec = matrix_weights(kernel_one, kernel_two, bias_one, gain_one, bias_two, gain_two)
    inside = build_interior(acc)
    f, e, ma, mb = build_field(inside, acc, rb0, rb1, ri0, ri1, m0, m1)
    ra = exchange(ma, LAT_OUTER)
    rb = exchange(mb, LAT_INNER)
    h = first_conv(f, e, w1, vec)
    return second_conv(h, ma, mb, ra, rb, w1, w2, vec)


def solution(mesh):
    placed = (
        P("lat", "lon", None, None, None),
        P("lat", "lon", None, None, None),
        P("lat", "lon", None),
        P("lat", "lon"),
        P("lat", "lon", None, None, None),
        P("lat", "lon", None, None, None),
        P("lat", "lon", None),
        P(),
        P(),
        P(),
        P(),
        P(),
        P(),
    )
    return jax.shard_map(
        local, mesh=mesh, in_specs=placed, out_specs=P("lat", "lon", None), check_vma=False
    )
```

```python
import jax
import jax.numpy as jnp
from jax import lax
from jax.experimental import pallas as pl
from jax.experimental.pallas import tpu as pltpu
from jax.sharding import PartitionSpec as P

F32 = jnp.float32
BF16 = jnp.bfloat16
BANDS = 4
SECTORS = 32
BIG = 24 << 20


def mesh_pairs(partner):
    return [
        (b * SECTORS + s, (lambda t: t[0] * SECTORS + t[1] % SECTORS)(partner(b, s)))
        for b in range(BANDS)
        for s in range(SECTORS)
    ]


LON_EVEN = mesh_pairs(lambda b, s: (b, s ^ 1))
LON_ODD = mesh_pairs(lambda b, s: (b, s + 1 if s % 2 else s - 1))
LAT_OUTER = mesh_pairs(
    lambda b, s: {0: (0, s + 16), 1: (2, s), 2: (1, s), 3: (3, s + 16)}[b]
)
LAT_INNER = mesh_pairs(lambda b, s: (b ^ 1, s))


def exchange(block, pairs):
    return lax.ppermute(block, ("lat", "lon"), pairs)


def nt_dot(a, b):
    return lax.dot_general(a, b, (((1,), (1,)), ((), ())), preferred_element_type=F32)


def group_ones(size, width):
    rows = lax.broadcasted_iota(jnp.int32, (size, size), 0) // width
    cols = lax.broadcasted_iota(jnp.int32, (size, size), 1) // width
    return (rows == cols).astype(F32).astype(BF16)


def norm_gelu(v, gain, ones, width):
    sq = v * v
    hi = sq.astype(BF16)
    lo = (sq - hi.astype(F32)).astype(BF16)
    total = jnp.dot(hi, ones, preferred_element_type=F32)
    total = total + jnp.dot(lo, ones, preferred_element_type=F32)
    x = v * lax.rsqrt(total * (1.0 / width) + 1e-05) * gain
    return jax.nn.gelu(x, approximate=True)


def unit(size):
    rows = lax.broadcasted_iota(jnp.int32, (size, size), 0)
    cols = lax.broadcasted_iota(jnp.int32, (size, size), 1)
    return (rows == cols).astype(F32).astype(BF16)


HBM = pl.BlockSpec(memory_space=pltpu.HBM)
SMEM = pl.BlockSpec(memory_space=pltpu.SMEM)
VMEM = pl.BlockSpec(memory_space=pltpu.VMEM)


def in_hbm(x):
    return pltpu.with_memory_space_constraint(x, pltpu.HBM)


def half_lanes():
    lanes = lax.broadcasted_iota(jnp.int32, (16, 128), 1)
    low = (lanes < 64).astype(F32).astype(BF16)
    high = (lanes >= 64).astype(F32).astype(BF16)
    return low, high


def send_sides(m0_ref, m1_ref, east, west):
    odd = lax.axis_index("lon") % 2

    def fill(east_ref, west_ref):
        for q in range(32):
            east_ref[q] = east(q).astype(BF16)
            west_ref[q] = west(q).astype(BF16)

    @pl.when(odd == 0)
    def _():
        fill(m0_ref, m1_ref)

    @pl.when(odd == 1)
    def _():
        fill(m1_ref, m0_ref)


def border_kernel(
    btarget_hbm, x_hbm, w_hbm, m0_ref, m1_ref, token, xv, wv, st, sb, acc, btarget, sem
):
    states = pltpu.make_async_copy(x_hbm, xv, sem.at[4])
    states.start()
    targets = pltpu.make_async_copy(btarget_hbm, btarget, sem.at[5])
    targets.start()
    chunks = [
        pltpu.make_async_copy(
            w_hbm.at[pl.ds(32 * c, 32)], wv.at[pl.ds(32 * c, 32)], sem.at[c]
        )
        for c in range(4)
    ]
    for c in chunks:
        c.start()
    acc[...] = jnp.zeros_like(acc)
    low, high = half_lanes()
    eye = unit(128)
    states.wait()
    for c in range(0, 16, 2):
        x = jnp.concatenate([xv[c], xv[c + 16], xv[c + 1], xv[c + 17]], axis=0)
        out = nt_dot(eye, x)
        st[pl.ds(c, 128, stride=16), :] = out[:, :128]
        st[pl.ds(c + 1, 128, stride=16), :] = out[:, 128:]
    for q in range(8):
        sb[16 * q : 16 * q + 16] = st[256 * q : 256 * q + 256].astype(BF16).reshape(16, 16, 128)
    targets.wait()
    for c in range(4):
        chunks[c].wait()

        def body(carry, c=c):
            n0 = 32 * c
            vals = []
            for u in range(0, 32, 2):
                rows = [sb[n0 + u + k] * half for k in range(2) for half in (low, high)]
                w = jnp.concatenate([wv[n0 + u], wv[n0 + u + 1]], axis=1)
                rhs = jnp.concatenate([w, w], axis=0)
                vals.append(
                    jnp.dot(jnp.concatenate(rows, axis=0), rhs, preferred_element_type=F32)
                )
            for u in range(32):
                k = u % 2
                acc[btarget[n0 + u]] += vals[u // 2][32 * k : 32 * k + 32, 128 * k : 128 * k + 128]
            return carry

        body(0)
    send_sides(m0_ref, m1_ref, lambda q: acc[32 + q], lambda q: acc[q])
    token[...] = jnp.zeros_like(token)


def border_sums(btarget, bstate, bweight):
    side = jax.ShapeDtypeStruct((32, 32, 128), BF16)
    return pl.pallas_call(
        border_kernel,
        name="border_sums",
        in_specs=[HBM, HBM, HBM],
        out_specs=[VMEM, VMEM, VMEM],
        out_shape=[side, side, jax.ShapeDtypeStruct((8, 128), F32)],
        scratch_shapes=[
            pltpu.VMEM((32, 64, 128), BF16),
            pltpu.VMEM((128, 64, 128), BF16),
            pltpu.VMEM((2048, 128), F32),
            pltpu.VMEM((128, 16, 128), BF16),
            pltpu.VMEM((64, 32, 128), F32),
            pltpu.SMEM((128,), jnp.int32),
            pltpu.SemaphoreType.DMA((6,)),
        ],
        cost_estimate=pl.CostEstimate(
            flops=2 * 128 * 32 * 64 * 128, bytes_accessed=4 << 20, transcendentals=0
        ),
        compiler_params=pltpu.CompilerParams(vmem_limit_bytes=BIG),
    )(in_hbm(btarget), in_hbm(jnp.transpose(bstate, (1, 2, 0))), in_hbm(bweight))


def sums_kernel(
    target, count_hbm, after, x_hbm, w_hbm, acc_ref, m0_ref, m1_ref,
    xv, wv, st, sb, live, xsem, wsem, lsem,
):
    states = [
        pltpu.make_async_copy(x_hbm.at[:, :, pl.ds(256 * p, 256)], xv.at[p], xsem.at[p])
        for p in range(2)
    ]
    chunks = {
        (p, c, h): pltpu.make_async_copy(
            w_hbm.at[pl.ds(256 * p + 128 * h + 32 * c, 32)],
            wv.at[pl.ds(256 * p + 128 * h + 32 * c, 32)],
            wsem.at[p, c, h],
        )
        for p in range(2)
        for c in range(4)
        for h in range(2)
    }
    for p in range(2):
        states[p].start()
    for c in chunks.values():
        c.start()
    counts = pltpu.make_async_copy(count_hbm, live, lsem)
    counts.start()
    low, high = half_lanes()
    low = jnp.concatenate([low, low], axis=0)
    high = jnp.concatenate([high, high], axis=0)
    eye = unit(128)
    for p in range(2):
        states[p].wait()
        for c in range(0, 32, 2):
            x = jnp.concatenate(
                [xv[p, c + k, :, 128 * h : 128 * h + 128] for k in range(2) for h in range(2)], axis=0
            )
            out = nt_dot(eye, x)
            st[pl.ds(c, 128, stride=32), :] = out[:, :128]
            st[pl.ds(c + 1, 128, stride=32), :] = out[:, 128:]
        for q in range(16):
            sb[128 * p + 8 * q : 128 * p + 8 * q + 8] = (
                st[256 * q : 256 * q + 256].astype(BF16).reshape(8, 32, 128)
            )
    counts.wait()
    count = live[0, 0]
    for p in range(2):
        for c in range(4):
            for h in range(2):
                chunks[p, c, h].wait()
        for u in range(0, 128, 2):
            rows = [sb[128 * p + u + k] * half for k in range(2) for half in (low, high)]
            cols = [[wv[256 * p + 128 * h + u + k] for k in range(2)] for h in range(2)]
            rhs = jnp.concatenate([jnp.concatenate(r, axis=1) for r in cols], axis=0)
            both = jnp.dot(jnp.concatenate(rows, axis=0), rhs, preferred_element_type=F32)
            for k in range(2):
                for h in range(2):
                    n = 256 * p + 128 * h + u + k
                    at = 64 * k + 32 * h
                    v = both[at : at + 32, 128 * k : 128 * k + 128]
                    if p == 0:
                        acc_ref[target[n]] = v
                    else:
                        acc_ref[jnp.where(n < count, target[n], 256)] += v
    send_sides(m0_ref, m1_ref, lambda q: acc_ref[8 * q + 7], lambda q: acc_ref[8 * q])


def inner_sums(target, count, after, state, weight):
    side = jax.ShapeDtypeStruct((32, 32, 128), BF16)
    return pl.pallas_call(
        sums_kernel,
        name="inner_sums",
        in_specs=[SMEM, HBM, VMEM, HBM, HBM],
        out_specs=[VMEM, VMEM, VMEM],
        out_shape=[pltpu.VMEM((257, 32, 128), F32), side, side],
        scratch_shapes=[
            pltpu.VMEM((2, 32, 64, 256), BF16),
            pltpu.VMEM((512, 64, 128), BF16),
            pltpu.VMEM((4096, 128), F32),
            pltpu.VMEM((256, 32, 128), BF16),
            pltpu.SMEM((1, 1), jnp.int32),
            pltpu.SemaphoreType.DMA((2,)),
            pltpu.SemaphoreType.DMA((2, 4, 2)),
            pltpu.SemaphoreType.DMA,
        ],
        cost_estimate=pl.CostEstimate(
            flops=2 * 512 * 32 * 64 * 128, bytes_accessed=16 << 20, transcendentals=0
        ),
        compiler_params=pltpu.CompilerParams(vmem_limit_bytes=BIG),
    )(target, count, after, in_hbm(jnp.transpose(state, (1, 2, 0))), in_hbm(weight))


def weights_kernel(k1_ref, k2_ref, b1_ref, g1_ref, b2_ref, g2_ref, w1_ref, w2_ref, v_ref):
    w1_ref[...] = jnp.zeros_like(w1_ref)
    w2_ref[...] = jnp.zeros_like(w2_ref)
    for r in range(7):
        for s in range(7):
            for t in range(4):
                row = r * 512 + (2 * t + s + 1) * 32
                w1_ref[row : row + 32, t * 64 : (t + 1) * 64] = k1_ref[r * 7 + s]
            for t in range(2):
                row = r * 640 + (2 * t + s + 1) * 64
                w2_ref[row : row + 64, t * 128 : (t + 1) * 128] = k2_ref[r * 7 + s]
    for t in range(4):
        v_ref[0:1, t * 64 : (t + 1) * 64] = b1_ref[...]
        v_ref[1:2, t * 64 : (t + 1) * 64] = g1_ref[...]
    for t in range(2):
        v_ref[2:3, t * 128 : (t + 1) * 128] = b2_ref[...]
        v_ref[3:4, t * 128 : (t + 1) * 128] = g2_ref[...]


def matrix_weights(k1, k2, b1, g1, b2, g2):
    return pl.pallas_call(
        weights_kernel,
        name="matrix_weights",
        out_shape=[
            jax.ShapeDtypeStruct((3584, 256), BF16),
            jax.ShapeDtypeStruct((4480, 256), BF16),
            jax.ShapeDtypeStruct((8, 256), F32),
        ],
        cost_estimate=pl.CostEstimate(flops=0, bytes_accessed=8 << 20, transcendentals=0),
        compiler_params=pltpu.CompilerParams(vmem_limit_bytes=16 << 20),
    )(k1.reshape(49, 32, 64), k2.reshape(49, 64, 128), b1[None], g1[None], b2[None], g2[None])


def selectors():
    rows = lax.broadcasted_iota(jnp.int32, (32, 128), 0)
    pix = lax.broadcasted_iota(jnp.int32, (32, 128), 1)
    pick = (pix // 4 == (rows % 8) * 4 + rows // 8).astype(F32).astype(BF16)
    keep = (
        lax.broadcasted_iota(jnp.int32, (128, 128), 0) // 32
        == lax.broadcasted_iota(jnp.int32, (128, 128), 1) % 4
    ).astype(F32).astype(BF16)
    return pick, keep


def place_pair(pair, pc0, y, fs, pick, keep, edge):
    spread = jnp.concatenate(
        [jnp.concatenate([v.astype(BF16)] * 4, axis=0) * keep for v in pair], axis=0
    )
    both = nt_dot(pick, spread)
    for h in range(2):
        pc = pc0 + h
        for k in range(4):
            v = both[8 * k : 8 * k + 8, 128 * h : 128 * h + 128]
            g = 2 * pc + k // 2
            kk = 4 * pc + k
            if 0 <= pc < 8:
                fs[y, k % 2, pl.ds(g, 8, stride=16), :] = v
            if k % 2 == 0 and 1 <= g <= 16:
                fs[y, 3, pl.ds(g - 1, 8, stride=16), :] = v
            if k % 2 == 1 and -1 <= g <= 14:
                fs[y, 2, pl.ds(g + 1, 8, stride=16), :] = v
            if kk in (-3, -2, -1, 0, 31, 32, 33):
                edge(kk + 3 if kk <= 0 else kk - 27, v)


def interior_kernel(acc, f_ref, fs):
    pick, keep = selectors()
    f_ref[:, 0:2] = jnp.zeros((4, 2, 2, 16, 128), BF16)
    f_ref[:, 130:132] = jnp.zeros((4, 2, 2, 16, 128), BF16)
    fs[...] = jnp.zeros_like(fs)

    def step(i, carry):
        for y in range(4):
            for c in range(1, 7, 2):
                pair = [acc[32 * i + 8 * y + c], acc[32 * i + 8 * y + c + 1]]
                place_pair(pair, c, y, fs, pick, keep, None)
            for a in range(4):
                f_ref[a, pl.ds(2 + 16 * i + 4 * y, 4)] = fs[y, a].astype(BF16).reshape(4, 2, 16, 128)
        return carry

    lax.fori_loop(0, 8, step, 0)


def build_interior(acc):
    return pl.pallas_call(
        interior_kernel,
        name="build_interior",
        in_specs=[VMEM],
        out_specs=VMEM,
        out_shape=pltpu.VMEM((4, 132, 2, 16, 128), BF16),
        scratch_shapes=[pltpu.VMEM((4, 4, 128, 128), F32)],
        cost_estimate=pl.CostEstimate(flops=1 << 28, bytes_accessed=8 << 20, transcendentals=0),
        compiler_params=pltpu.CompilerParams(vmem_limit_bytes=16 << 20),
    )(acc)


def field_kernel(
    inside, acc, rb0_ref, rb1_ref, ri0_ref, ri1_ref, m0_ref, m1_ref,
    f_ref, e_ref, ma_ref, mb_ref, fs, et,
):
    odd = lax.axis_index("lon") % 2
    upper = lax.axis_index("lat") % 2
    pick, keep = selectors()
    et[...] = jnp.zeros_like(et)
    fs[...] = jnp.zeros_like(fs)
    is_odd = odd == 1

    def step(i, carry):
        for y in range(4):
            n = 4 * i + y
            east_border = jnp.where(is_odd, rb1_ref[n], rb0_ref[n]).astype(F32)
            east_inner = jnp.where(is_odd, ri1_ref[n], ri0_ref[n]).astype(F32)
            west_border = jnp.where(is_odd, rb0_ref[n], rb1_ref[n]).astype(F32)
            west_inner = jnp.where(is_odd, ri0_ref[n], ri1_ref[n]).astype(F32)
            own_east = jnp.where(is_odd, m1_ref[n], m0_ref[n]).astype(F32)
            own_west = jnp.where(is_odd, m0_ref[n], m1_ref[n]).astype(F32)

            def edge(slot, v, y=y):
                e_ref[slot, pl.ds(8 + 32 * i + 8 * y, 8), :] = v
                et[y, pl.ds(slot, 8, stride=16), :] = v

            west = [west_inner + own_west, acc[8 * n] + west_border]
            east = [acc[8 * n + 7] + east_border, east_inner + own_east]
            place_pair(west, -1, y, fs, pick, keep, edge)
            place_pair(east, 7, y, fs, pick, keep, edge)
            for a in range(4):
                to = pl.ds(2 + 16 * i + 4 * y, 4)
                f_ref[a, to] = inside[a, to] + fs[y, a].astype(BF16).reshape(4, 2, 16, 128)

        def send(ref, first, start):
            for a in range(4):
                ref[a] = f_ref[a, 2 + start + first : 2 + start + first + 5]
            for q in range(5):
                y, o = (first + q) // 4, (first + q) % 4
                ref[4, q] = et[y, 32 * o : 32 * o + 32].astype(BF16).reshape(2, 16, 128)

        @pl.when((i == 0) & (upper == 0))
        def _():
            send(ma_ref, 0, 0)

        @pl.when((i == 0) & (upper == 1))
        def _():
            send(mb_ref, 0, 0)

        @pl.when((i == 7) & (upper == 0))
        def _():
            send(mb_ref, 11, 112)

        @pl.when((i == 7) & (upper == 1))
        def _():
            send(ma_ref, 11, 112)

        return carry

    lax.fori_loop(0, 8, step, 0)


def build_field(inside, acc, *sides):
    msg = jax.ShapeDtypeStruct((5, 5, 2, 16, 128), BF16)
    return pl.pallas_call(
        field_kernel,
        name="build_field",
        in_specs=[VMEM] * 8,
        out_specs=[VMEM] * 4,
        out_shape=[
            pltpu.VMEM((4, 132, 2, 16, 128), BF16),
            pltpu.VMEM((7, 272, 128), F32),
            msg,
            msg,
        ],
        input_output_aliases={0: 0},
        scratch_shapes=[
            pltpu.VMEM((4, 4, 128, 128), F32),
            pltpu.VMEM((4, 128, 128), F32),
        ],
        compiler_params=pltpu.CompilerParams(vmem_limit_bytes=16 << 20),
    )(inside, acc, *sides)


ORDER = (2, 0, 1, 3)


TILE = 32


def first_kernel(f_ref, e_ref, w_ref, v_ref, h_ref, raw, edge, hs, ms, el):
    ones = group_ones(256, 64)
    many = TILE * 16
    tiles = 128 // TILE

    def mix(lhs):
        return jnp.dot(lhs, w_ref[...], preferred_element_type=F32) + v_ref[0:1]

    def side(n):
        parts = []
        for r in range(7):
            for j in range(4):
                slot = 4 * n + j
                if slot == 7:
                    parts.append(jnp.zeros((128, 128), BF16))
                else:
                    parts.append(e_ref[slot, pl.ds(8 - 3 + r, 128, stride=2), :].astype(BF16))
        return jnp.concatenate(parts, axis=1)

    def start(i):
        parts = []
        for r in range(7):
            for a in ORDER:
                first = TILE * i + (r + 1) // 2
                x = f_ref[a, first : first + TILE, (r + 1) % 2]
                parts.append(x.reshape(many, 128))
        raw[i] = mix(jnp.concatenate(parts, axis=1))

    def finish(i):
        h = norm_gelu(raw[i], v_ref[1:2], ones, 64)
        for c in range(2):
            hs[i, c, 8 : 8 + many] = h[:, 128 * c : 128 * c + 128]
        ms[i, 0] = hs[i, 0, 7 : 7 + many]
        ms[i, 1] = hs[i, 1, 7 : 7 + many]
        ms[i, 2] = hs[i, 0, 9 : 9 + many]
        rows = slice(TILE * i, TILE * i + TILE)
        ms[i, 0, pl.ds(0, TILE, stride=16), :] = el[0, rows, 0:128]
        ms[i, 1, pl.ds(0, TILE, stride=16), :] = el[0, rows, 128:256]
        ms[i, 2, pl.ds(15, TILE, stride=16), :] = el[1, rows, 0:128]
        half = TILE // 2
        tile = lambda v: v.astype(BF16).reshape(half, 2, 16, 128)
        to = slice(half * i, half * i + half)
        h_ref[0, to] = tile(ms[i, 0])
        h_ref[1, to] = tile(ms[i, 1])
        h_ref[2, to] = tile(hs[i, 0, 8 : 8 + many])
        h_ref[3, to] = tile(hs[i, 1, 8 : 8 + many])
        h_ref[4, to] = tile(ms[i, 2])

    edge[...] = mix(jnp.concatenate([side(0), side(1)], axis=0))
    start(0)
    out = norm_gelu(edge[...], v_ref[1:2], ones, 64)
    el[0] = out[0:128]
    el[1] = out[128:256]
    for i in range(tiles):
        if i + 1 < tiles:
            start(i + 1)
        finish(i)


def first_conv(f, e, w1, vec):
    tiles = 128 // TILE
    many = TILE * 16
    return pl.pallas_call(
        first_kernel,
        name="first_conv",
        in_specs=[VMEM] * 4,
        out_specs=VMEM,
        out_shape=pltpu.VMEM((5, 64, 2, 16, 128), BF16),
        scratch_shapes=[
            pltpu.VMEM((tiles, many, 256), F32),
            pltpu.VMEM((256, 256), F32),
            pltpu.VMEM((tiles, 2, many + 16, 128), F32),
            pltpu.VMEM((tiles, 3, many, 128), F32),
            pltpu.VMEM((2, 128, 256), F32),
        ],
        cost_estimate=pl.CostEstimate(
            flops=2 * 2304 * 3584 * 256, bytes_accessed=12 << 20, transcendentals=1 << 20
        ),
        compiler_params=pltpu.CompilerParams(vmem_limit_bytes=28 << 20),
    )(f, e, w1, vec)


BASES = (0, 2, 4, 11, 13, 20, 27, 29)


def second_kernel(
    h_ref, ma_ref, mb_ref, ra_ref, rb_ref, w1_ref, w2_ref, v_ref,
    o_ref, top, bot, ve, vf, le, ts, ms, raw, os,
):
    lat = lax.axis_index("lat")
    odd = lat % 2 == 1
    north = lat == 0
    south = lat == 3
    ones1 = group_ones(256, 64)
    ones2 = group_ones(256, 128)

    def window(ref, first, count):
        parts = []
        for r in range(7):
            for a in range(5):
                at = first + (r + 1) // 2
                parts.append(ref[a, at : at + count, (r + 1) % 2].reshape(16 * count, 128))
        return jnp.concatenate(parts, axis=1)

    def mix(lhs):
        return jnp.dot(lhs, w2_ref[...], preferred_element_type=F32) + v_ref[2:3]

    def finish(n, at, first, count):
        y = norm_gelu(raw[n, at : at + 16 * count], v_ref[3:4], ones2, 128)
        for t in range(2):
            os[n, pl.ds(2 * at + t, 16 * count, stride=2), :] = y[:, 128 * t : 128 * t + 128]
        o_ref[first : first + count] = (
            os[n, 2 * at : 2 * at + 32 * count].astype(BF16).reshape(count, 32, 128)
        )

    def row(ref, a, m):
        return ref[a, m // 2, m % 2]

    def own_top(a, m):
        return jnp.where(odd, row(mb_ref, a, m), row(ma_ref, a, m))

    def own_bot(a, m):
        return jnp.where(odd, row(ma_ref, a, m), row(mb_ref, a, m))

    def halo_top(a, m):
        return jnp.where(odd, row(rb_ref, a, m), row(ra_ref, a, m))

    def halo_bot(a, m):
        return jnp.where(odd, row(ra_ref, a, m), row(rb_ref, a, m))

    for a in range(5):
        def put(n, v):
            if a < 4:
                vf[a, n] = v
            else:
                ve[16 * n : 16 * n + 16] = v.astype(F32)

        for q in range(11):
            normal = halo_top(a, q + 1) if q < 9 else own_top(a, q - 9)
            polar = own_top(a, 2 - q) if q < 3 else halo_top(a, q - 3)
            put(q, jnp.where(north, polar, normal))
        for q in range(9):
            if q < 3:
                v = jnp.where(north, halo_top(a, 2 - q), halo_top(a, 7 + q))
            else:
                v = own_top(a, q - 3)
            put(11 + q, v)
        for q in range(7):
            if q < 5:
                v = own_bot(a, 5 + q)
            else:
                v = jnp.where(south, halo_bot(a, 14 - q), halo_bot(a, q - 5))
            put(20 + q, v)
        for q in range(9):
            normal = own_bot(a, 7 + q) if q < 3 else halo_bot(a, q - 3)
            polar = halo_bot(a, 3 + q) if q < 7 else own_bot(a, 16 - q)
            put(27 + q, jnp.where(south, polar, normal))

    for n, base in enumerate(BASES):
        for r in range(7):
            for j in range(4):
                col = 128 * (4 * r + j)
                for side in range(2):
                    src = 16 * (base + r) + 4 * side + j
                    le[n + 8 * side : n + 8 * side + 1, col : col + 128] = ve[src : src + 1, :]
    parts = []
    for r in range(7):
        for a in ORDER:
            parts.append(jnp.concatenate([vf[a, base + r] for base in BASES], axis=0))
    lhs = jnp.concatenate([jnp.concatenate(parts, axis=1), le[...].astype(BF16)], axis=0)
    ts[2] = jnp.dot(lhs, w1_ref[...], preferred_element_type=F32) + v_ref[0:1]
    raw[0] = mix(window(h_ref, 14, 32))
    for a in range(5):
        top[a, 2:20] = h_ref[a, 0:18]
        bot[a, 0:18] = h_ref[a, 46:64]
    h = norm_gelu(ts[2], v_ref[1:2], ones1, 64)
    for c in range(2):
        ts[c, 8:136, 0:128] = h[0:128, 128 * c : 128 * c + 128]
    ms[0] = ts[0, 7:135, 0:128]
    ms[1] = ts[1, 7:135, 0:128]
    ms[2] = ts[0, 9:137, 0:128]
    ms[0, pl.ds(0, 8, stride=16), :] = h[128:136, 0:128]
    ms[1, pl.ds(0, 8, stride=16), :] = h[128:136, 128:256]
    ms[2, pl.ds(15, 8, stride=16), :] = h[136:144, 0:128]
    full = [ms[0], ms[1], ts[0, 8:136, 0:128], ts[1, 8:136, 0:128], ms[2]]
    for a in range(5):
        v = full[a].astype(BF16).reshape(8, 16, 128)
        top[a, 0, 1] = jnp.where(north, v[2], v[0])
        top[a, 1, 0] = v[1]
        top[a, 1, 1] = jnp.where(north, v[0], v[2])
        top[a, 2, 0] = v[3]
        top[a, 2, 1] = v[4]
        bot[a, 17, 1] = v[5]
        bot[a, 18, 0] = jnp.where(south, v[7], v[6])
        bot[a, 18, 1] = jnp.where(south, v[6], v[7])
    raw[1] = mix(jnp.concatenate([window(top, 0, 16), window(bot, 0, 16)], axis=0))
    finish(0, 0, 16, 32)
    finish(1, 0, 0, 16)
    finish(1, 256, 48, 16)


def second_conv(h, ma, mb, ra, rb, w1, w2, vec):
    return pl.pallas_call(
        second_kernel,
        name="second_conv",
        in_specs=[VMEM] * 8,
        out_specs=VMEM,
        out_shape=jax.ShapeDtypeStruct((64, 32, 128), BF16),
        scratch_shapes=[
            pltpu.VMEM((5, 20, 2, 16, 128), BF16),
            pltpu.VMEM((5, 20, 2, 16, 128), BF16),
            pltpu.VMEM((36 * 16, 128), F32),
            pltpu.VMEM((4, 36, 16, 128), BF16),
            pltpu.VMEM((16, 3584), F32),
            pltpu.VMEM((3, 144, 256), F32),
            pltpu.VMEM((3, 128, 128), F32),
            pltpu.VMEM((2, 512, 256), F32),
            pltpu.VMEM((2, 1024, 128), F32),
        ],
        compiler_params=pltpu.CompilerParams(vmem_limit_bytes=28 << 20),
    )(h, ma, mb, ra, rb, w1, w2, vec)


def local(
    cell_state,
    remap_weight,
    block_target,
    block_count,
    border_state,
    border_weight,
    border_target,
    kernel_one,
    bias_one,
    gain_one,
    kernel_two,
    bias_two,
    gain_two,
):
    m0, m1, after = border_sums(border_target[0, 0], border_state[0, 0], border_weight[0, 0])
    rb0 = exchange(m0, LON_EVEN)
    rb1 = exchange(m1, LON_ODD)
    acc, i0, i1 = inner_sums(
        block_target[0, 0], block_count, after, cell_state[0, 0], remap_weight[0, 0]
    )
    ri0 = exchange(i0, LON_EVEN)
    ri1 = exchange(i1, LON_ODD)
    w1, w2, vec = matrix_weights(kernel_one, kernel_two, bias_one, gain_one, bias_two, gain_two)
    inside = build_interior(acc)
    f, e, ma, mb = build_field(inside, acc, rb0, rb1, ri0, ri1, m0, m1)
    ra = exchange(ma, LAT_OUTER)
    rb = exchange(mb, LAT_INNER)
    h = first_conv(f, e, w1, vec)
    return second_conv(h, ma, mb, ra, rb, w1, w2, vec)


def solution(mesh):
    placed = (
        P("lat", "lon", None, None, None),
        P("lat", "lon", None, None, None),
        P("lat", "lon", None),
        P("lat", "lon"),
        P("lat", "lon", None, None, None),
        P("lat", "lon", None, None, None),
        P("lat", "lon", None),
        P(),
        P(),
        P(),
        P(),
        P(),
        P(),
    )
    return jax.shard_map(
        local, mesh=mesh, in_specs=placed, out_specs=P("lat", "lon", None), check_vma=False
    )
```
